256 devices in a mesh: section: 64 (over z, y, core), tensor: 4 (over x).
Axes of the slice: x: 4, y: 4, z: 8, core: 2. Of those that a mesh axis runs over, the one named last changes fastest.
Arguments:
- inner_input: bfloat16 [2, 2048, 8192], P(None, 'section', 'tensor'), may hold values from -6 to 6
- gate_input: bfloat16 [2, 2048, 8192], P(None, 'section', 'tensor'), may hold values from -6 to 6
- conv_state: bfloat16 [2048, 3, 8192], P('section', None, 'tensor'), may hold values from -6 to 6
- mamba_state: bfloat16 [2048, 16, 8192], P('section', None, 'tensor'), may hold values from -6 to 6
- conv_weight: float32 [4, 8192], P(None, 'tensor'), may hold values from -3 to 3
- conv_bias: float32 [8192], P('tensor'), may hold values from -0.5 to 0.5
- xproj_weight: bfloat16 [544, 8192], P(None, 'tensor'), may hold values from -0.0625 to 0.0625
- dt_gain: float32 [512], replicated, may hold values from 0.5 to 1.5
- dtproj_weight: bfloat16 [512, 8192], P(None, 'tensor'), may hold values from -0.25 to 0.25
- dt_bias: float32 [8192], P('tensor'), may hold values from -4 to -1
- decay_rate: float32 [16, 8192], P(None, 'tensor'), may hold values from 0.05 to 2
- skip_gain: float32 [8192], P('tensor'), may hold values from 0.5 to 1.5
- query: bfloat16 [2, 2048, 8192], P(None, 'section', 'tensor'), may hold values from -14 to 14
- key_cache: bfloat16 [2048, 32, 1024], P('section', None, 'tensor'), may hold values from -6 to 6
- value_cache: bfloat16 [2048, 32, 1024], P('section', None, 'tensor'), may hold values from -6 to 6
- key_new: bfloat16 [2, 2048, 1024], P(None, 'section', 'tensor'), may hold values from -6 to 6
- value_new: bfloat16 [2, 2048, 1024], P(None, 'section', 'tensor'), may hold values from -6 to 6
- kv_length: int32 [2048], P('section'), may hold values from 2 to 30, as said below
- new_owner: int32 [2048], replicated, may hold values from 0 to 63, as said below
Outputs:
- mamba_out: bfloat16 [2, 2048, 8192], P(None, 'section', 'tensor')
- attn_out: bfloat16 [2, 2048, 8192], P(None, 'section', 'tensor')
- moved_conv: bfloat16 [2048, 3, 8192], P('section', None, 'tensor')
- moved_state: bfloat16 [2048, 16, 8192], P('section', None, 'tensor')
- moved_keys: bfloat16 [2048, 32, 1024], P('section', None, 'tensor')
- moved_values: bfloat16 [2048, 32, 1024], P('section', None, 'tensor')
The draws below stay inside these ranges and needn't reach their ends.
Inputs may be any that keep to these rules, and one draw needn't show every extreme that they name: `new_owner`: for every local slot number j, each section index receives exactly one request that stands in slot j of some section index, and it takes slot j; one section index sends at most 1 request to one section index, and some pairs reach 1. `kv_length`: some request has each bound.
All inputs are finite; a program needn't handle non-finite values.
Results may differ from the reference program's by a relative error of at most 0.0052.
Values may be sent and summed in bfloat16 or wider, within the bound.
A program may use at most 128 MiB of HBM per device.

```python
import math
import jax
import jax.numpy as jnp
from jax import lax

INNER = 8192
STATE = 16
CONV = 4
DT_RANK = 512
HEADS = 64
KV_HEADS = 8
HEAD = 128
STEPS = 2
R_DEV = 32
CACHE = 32
REQUESTS = 2048
N_SECTION = 64


def cache_pair(key):
    base = jax.random.fold_in(key, 17)
    key_part = jax.random.fold_in(base, 1)
    query_part = jax.random.fold_in(base, 2)
    key_values = jnp.clip(jax.random.normal(key_part, (REQUESTS, CACHE, KV_HEADS * HEAD), jnp.float32), -6.0, 6.0)
    query_values = jnp.clip(jax.random.normal(query_part, (STEPS, REQUESTS, HEADS * HEAD), jnp.float32), -6.0, 6.0)
    return (query_values, key_values)


def draw_query(key, part):
    return cache_pair(key)[0].astype(jnp.bfloat16)


def draw_key_cache(key, part):
    return cache_pair(key)[1].astype(jnp.bfloat16)


def draw_kv_length(key, part):
    longest = CACHE - STEPS
    lengths = jax.random.randint(jax.random.fold_in(key, 41), (REQUESTS,), 2, longest + 1)
    first_row = jax.random.randint(jax.random.fold_in(key, 42), (), 0, REQUESTS)
    second_row = (first_row + 1 + jax.random.randint(jax.random.fold_in(key, 43), (), 0, REQUESTS - 1)) % REQUESTS
    lengths = lengths.at[first_row].set(longest).at[second_row].set(2)
    return lengths.astype(jnp.int32)


def draw_new_owner(key, part):
    section_count = REQUESTS // R_DEV
    residues = jax.random.permutation(jax.random.fold_in(key, 51), section_count)
    shuffle = jax.random.permutation(jax.random.fold_in(key, 52), R_DEV)
    relabel = jax.random.permutation(jax.random.fold_in(key, 53), section_count)
    offsets = residues[shuffle % section_count]
    request_ids = jnp.arange(REQUESTS, dtype=jnp.int32)
    source_section = request_ids // R_DEV
    local_slot = request_ids % R_DEV
    return relabel[(source_section + offsets[local_slot]) % section_count].astype(jnp.int32)


def levels(own_key, shape, shards, least, top_value):
    loudness, own = 1.0, jax.random.fold_in(own_key, 6)
    for axis_at, blocks in shards:
        heights = jnp.exp(jax.random.uniform(jax.random.fold_in(own, axis_at), (blocks,), jnp.float32, least / len(shards), top_value / len(shards)))
        loudness = loudness * jnp.repeat(heights, shape[axis_at] // blocks).reshape([-1 if axis == axis_at else 1 for axis in range(len(shape))])
    return loudness


def gaussian(own_key, shape, deviation, most, cuts=(), held_as=jnp.bfloat16):
    gain = levels(own_key, shape, cuts, -0.22, 0.18) if cuts else 1.0
    drawn = jax.random.normal(own_key, shape, jnp.float32) * deviation * gain
    return jnp.minimum(jnp.maximum(drawn, -most), most).astype(held_as)


def setup_inputs(seed: int = 0) -> dict:
    seeds = jax.random.split(jax.random.key(seed), 20)
    return {
        "inner_input": gaussian(seeds[0], (STEPS, REQUESTS, INNER), 1.0, 6.0, ((1, 64), (2, 4))),
        "gate_input": gaussian(seeds[1], (STEPS, REQUESTS, INNER), 1.0, 6.0, ((1, 64), (2, 4))),
        "conv_state": gaussian(seeds[2], (REQUESTS, CONV - 1, INNER), 1.0, 6.0, ((0, 64), (2, 4))),
        "mamba_state": gaussian(seeds[3], (REQUESTS, STATE, INNER), 1.0, 6.0, ((0, 64), (2, 4))),
        "conv_weight": gaussian(seeds[4], (CONV, INNER), CONV ** -0.5, 3.0, ((1, 4),), jnp.float32),
        "conv_bias": jnp.clip(jax.random.uniform(seeds[5], (INNER,), jnp.float32, -0.5, 0.5) * levels(seeds[5], (INNER,), ((0, 4),), -0.4, 0.0), -0.5, 0.5),
        "xproj_weight": gaussian(seeds[6], (DT_RANK + 2 * STATE, INNER), INNER ** -0.5, 0.0625, ((1, 4),)),
        "dt_gain": jnp.clip(jax.random.uniform(seeds[7], (DT_RANK,), jnp.float32, 0.5, 1.5), 0.5, 1.5),
        "dtproj_weight": gaussian(seeds[8], (DT_RANK, INNER), DT_RANK ** -0.5, 0.25, ((1, 4),)),
        "dt_bias": jnp.clip(-4.0 + 3.0 * jax.random.uniform(seeds[9], (INNER,), jnp.float32) ** levels(seeds[9], (INNER,), ((0, 4),), -0.2, 0.2), -4.0, -1.0),
        "decay_rate": jnp.clip(jnp.exp(math.log(2.0) - 3.6888794 * jax.random.uniform(seeds[10], (STATE, INNER), jnp.float32) ** levels(seeds[10], (STATE, INNER), ((1, 4),), -0.2, 0.2)), 0.05, 2.0),
        "skip_gain": jnp.clip(0.5 + 1.0 * jax.random.uniform(seeds[11], (INNER,), jnp.float32) ** levels(seeds[11], (INNER,), ((0, 4),), -0.2, 0.2), 0.5, 1.5),
        "query": draw_query(jax.random.fold_in(seeds[19], 71), 0),
        "key_cache": draw_key_cache(jax.random.fold_in(seeds[19], 71), 0),
        "value_cache": gaussian(seeds[14], (REQUESTS, CACHE, KV_HEADS * HEAD), 1.0, 6.0, ((0, 64), (2, 4))),
        "key_new": gaussian(seeds[15], (STEPS, REQUESTS, KV_HEADS * HEAD), 1.0, 6.0, ((1, 64), (2, 4))),
        "value_new": gaussian(seeds[16], (STEPS, REQUESTS, KV_HEADS * HEAD), 1.0, 6.0, ((1, 64), (2, 4))),
        "kv_length": draw_kv_length(jax.random.fold_in(seeds[19], 71), 0),
        "new_owner": draw_new_owner(jax.random.fold_in(seeds[19], 71), 0),
    }


epsilon = 1e-06

def reference(inner_input, gate_input, conv_state, mamba_state, conv_weight, conv_bias, xproj_weight, dt_gain, dtproj_weight, dt_bias, decay_rate, skip_gain, query, key_cache, value_cache, key_new, value_new, kv_length, new_owner):
    window = jnp.concatenate([conv_state, jnp.swapaxes(inner_input, 0, 1)], axis=1)
    conv_list = []
    for step_index in range(STEPS):
        summed = jnp.zeros((REQUESTS, INNER), jnp.float32) + conv_bias
        for tap_index in range(CONV):
            summed = summed + conv_weight[tap_index] * window[:, step_index + tap_index].astype(jnp.float32)
        conv_list.append(jax.nn.silu(summed).astype(jnp.bfloat16))
    conv_out = jnp.stack(conv_list)
    projected = lax.dot_general(conv_out.reshape(STEPS * REQUESTS, INNER), xproj_weight, (((1,), (1,)), ((), ())), preferred_element_type=jnp.float32).reshape(STEPS, REQUESTS, DT_RANK + 2 * STATE)
    low_rank = projected[..., :DT_RANK]
    scaled = (low_rank * lax.rsqrt(lax.optimization_barrier(jnp.mean(low_rank * low_rank, axis=-1, keepdims=True)) + epsilon) * dt_gain).astype(jnp.bfloat16)
    delta_rate = jax.nn.softplus(jnp.dot(scaled.reshape(STEPS * REQUESTS, DT_RANK), dtproj_weight, preferred_element_type=jnp.float32).reshape(STEPS, REQUESTS, INNER) + dt_bias)
    input_gain = projected[..., DT_RANK:DT_RANK + STATE]
    output_gain = projected[..., DT_RANK + STATE:]

    def blocked(source_array):
        swapped = jnp.swapaxes(source_array, 0, 1)
        return swapped.reshape((N_SECTION, R_DEV) + swapped.shape[1:])

    def recurrence(pieces):
        state_in, delta_block, gain_in, gain_out, conv_block, gate_block = pieces
        hidden = state_in.astype(jnp.float32)
        results = []
        for step_index in range(STEPS):
            step_rate = delta_block[:, step_index]
            inputs_now = conv_block[:, step_index].astype(jnp.float32)
            hidden = jnp.exp(-step_rate[:, None, :] * decay_rate[None]) * hidden + (step_rate * inputs_now)[:, None, :] * gain_in[:, step_index, :, None]
            reading = lax.optimization_barrier(jnp.sum(hidden * gain_out[:, step_index, :, None], axis=1)) + skip_gain * inputs_now
            results.append((reading * jax.nn.silu(gate_block[:, step_index].astype(jnp.float32))).astype(jnp.bfloat16))
        return (jnp.stack(results, axis=1), hidden.astype(jnp.bfloat16))
    outputs, final_state = lax.map(recurrence, (mamba_state.reshape(N_SECTION, R_DEV, STATE, INNER), blocked(delta_rate), blocked(input_gain), blocked(output_gain), blocked(conv_out), blocked(gate_input)))
    mamba_out = jnp.swapaxes(outputs.reshape(REQUESTS, STEPS, INNER), 0, 1)
    final_state = final_state.reshape(REQUESTS, STATE, INNER)
    final_conv = window[:, STEPS:]
    positions = jnp.arange(CACHE, dtype=jnp.int32)
    group_size = HEADS // KV_HEADS
    key_rows = key_cache
    value_rows = value_cache
    attended = []
    for step_index in range(STEPS):
        target = kv_length + step_index
        written = (positions[None, :] == target[:, None])[:, :, None]
        key_rows = jnp.where(written, key_new[step_index][:, None, :], key_rows)
        value_rows = jnp.where(written, value_new[step_index][:, None, :], value_rows)
        queries = query[step_index].astype(jnp.float32).reshape(REQUESTS, KV_HEADS, group_size, HEAD)
        key_heads = key_rows.astype(jnp.float32).reshape(REQUESTS, CACHE, KV_HEADS, HEAD)
        scores = jnp.einsum('rgqd,rcgd->rgqc', queries, key_heads) / math.sqrt(HEAD)
        allowed = (positions[None, :] <= target[:, None])[:, None, None, :]
        scores = jnp.where(allowed, scores, -1e+30)
        highest = lax.optimization_barrier(jnp.max(scores, axis=-1, keepdims=True))
        weights = jnp.exp(scores - highest)
        weights = (weights / lax.optimization_barrier(jnp.sum(weights, axis=-1, keepdims=True))).astype(jnp.bfloat16)
        value_heads = value_rows.astype(jnp.float32).reshape(REQUESTS, CACHE, KV_HEADS, HEAD)
        mixed_out = jnp.einsum('rgqc,rcgd->rgqd', weights.astype(jnp.float32), value_heads)
        attended.append(mixed_out.reshape(REQUESTS, HEADS * HEAD).astype(jnp.bfloat16))
    destination = new_owner.astype(jnp.int32) * R_DEV + jnp.arange(REQUESTS, dtype=jnp.int32) % R_DEV

    def relocate(source_array):
        return jnp.zeros_like(source_array).at[destination].set(source_array)
    return (mamba_out, jnp.stack(attended), relocate(final_conv), relocate(final_state), relocate(key_rows), relocate(value_rows))
```

```python
import functools
import math

import jax
import jax.numpy as jnp
from jax import lax
from jax.experimental import pallas as pl
from jax.experimental.pallas import tpu as pltpu
from jax.sharding import PartitionSpec as P

HEAD = 128
MESH = pl.DeviceIdType.MESH
PLANES = 8
RANKS = 8
CAPS = (120, 96, 68, 36)


epsilon = 1e-06


def project_rows(conv_rows, xproj_weight):
    return lax.dot_general(
        conv_rows, xproj_weight, (((1,), (1,)), ((), ())), preferred_element_type=jnp.float32
    )


def route_tables(new_owner, plane):
    requests_here = new_owner.shape[0] // (PLANES * RANKS)
    width = RANKS * requests_here
    owner = new_owner.reshape(PLANES, width)
    own_plane = jnp.arange(PLANES, dtype=jnp.int32)[:, None]
    packet = jnp.arange(width, dtype=jnp.int32)[None, :]
    away = (owner // RANKS - own_plane) % PLANES
    kind = jnp.where(away == 0, 7, jnp.where(away == 4, 0, jnp.where(away < 4, 4 - away, away - 1)))
    key = kind * width + packet
    rank = jnp.sum((key[:, None, :] < key[:, :, None]).astype(jnp.int32), axis=-1)
    count = [jnp.sum((kind == k).astype(jnp.int32), axis=-1, keepdims=True) for k in range(7)]
    ties = count[0]
    ups = count[1] + count[2] + count[3]
    downs = count[4] + count[5] + count[6]
    ties_up = jnp.clip((ups + ties + downs + 1) // 2 - ups, 0, ties)
    ties_down = ties - ties_up
    goes_up = jnp.where(kind == 0, rank < ties_up, kind <= 3)
    place = jnp.where(
        kind == 0,
        jnp.where(rank < ties_up, rank, rank - ties_up),
        jnp.where(kind <= 3, rank - ties + ties_up, rank - ties - ups + ties_down),
    )
    hops = jnp.where(kind == 0, 4, jnp.where(kind <= 3, 4 - kind, 7 - kind))
    starts = [0, CAPS[0], CAPS[0] + CAPS[1], CAPS[0] + CAPS[1] + CAPS[2]]
    start = jnp.where(hops == 1, starts[0], jnp.where(hops == 2, starts[1], jnp.where(hops == 3, starts[2], starts[3])))
    arrival = start + place + jnp.where(goes_up, 0, sum(CAPS))
    fits = jnp.array(True)
    for ties_here, near in ((ties_up, count[1:4]), (ties_down, count[4:7])):
        load = ties_here
        for hop in (3, 2, 1, 0):
            fits = fits & jnp.all(load <= CAPS[hop])
            if hop:
                load = load + near[3 - hop]
    pick = lambda rows: lax.dynamic_slice_in_dim(rows, plane, 1, 0)[0]
    my_kind, my_up, my_place = pick(kind), pick(goes_up.astype(jnp.int32)), pick(place)
    lane = jnp.where(my_kind == 7, -1, my_place + jnp.where(my_up == 1, 0, CAPS[0]))
    slots = jnp.arange(2 * CAPS[0], dtype=jnp.int32)
    lane = jnp.where((my_up == 1) & (my_place >= CAPS[0]), -1, lane)
    send = jnp.sum(jnp.where(lane[None, :] == slots[:, None], packet, 0), axis=-1)
    coded = jnp.where(kind == 7, packet + 65536, arrival).reshape(PLANES * RANKS, 1, requests_here)
    mine = plane * RANKS + jnp.arange(RANKS, dtype=jnp.int32)
    landed = new_owner.reshape(PLANES * RANKS, 1, requests_here) == mine[None, :, None]
    found = jnp.sum(jnp.where(landed, coded, 0), axis=0).reshape(width)
    stays = found >= 65536
    return (
        fits,
        send,
        jnp.where(stays, found - 65536, 0),
        jnp.where(stays, 0, found),
        stays.astype(jnp.int32),
    )


def migrate_kernel(count, send_tab, stay_tab, land_tab, flag_tab, *refs):
    parts = refs[:count]
    outs = refs[count : 2 * count]
    spread = refs[2 * count : 3 * count]
    queue = refs[3 * count : 4 * count]
    ring = refs[4 * count : 5 * count]
    gathered = refs[5 * count : 6 * count]
    a_send, a_recv, a_self, z_send, z_recv, c_send, c_recv, c_self = refs[6 * count :]
    section = lax.axis_index("section")
    tensor = lax.axis_index("tensor")
    plane = section // RANKS
    me = section % RANKS
    width = spread[0].shape[0]
    each = width // RANKS
    up = lax.rem(plane + 1, PLANES) * RANKS + me
    down = lax.rem(plane + PLANES - 1, PLANES) * RANKS + me
    peers = [lax.rem(me + o, RANKS) for o in range(RANKS)]
    partner = [(plane * RANKS + p, tensor) for p in peers]

    barrier = pltpu.get_barrier_semaphore()
    for device in [partner[o] for o in range(1, RANKS)] + [(up, tensor), (down, tensor)]:
        pl.semaphore_signal(barrier, inc=1, device_id=device, device_id_type=MESH)
    pl.semaphore_wait(barrier, RANKS + 1)

    def spread_copy(k, o):
        return pltpu.make_async_remote_copy(
            src_ref=parts[k].at[peers[o]],
            dst_ref=spread[k].at[pl.ds(me * each, each)],
            send_sem=a_send.at[k, o],
            recv_sem=a_recv.at[k, o],
            device_id=partner[o],
            device_id_type=MESH,
        )

    def spread_self(k):
        return pltpu.make_async_copy(parts[k].at[me], spread[k].at[pl.ds(me * each, each)], a_self.at[k])

    starts = [0, CAPS[0], CAPS[0] + CAPS[1], CAPS[0] + CAPS[1] + CAPS[2]]

    def ring_copy(k, d, h):
        base = d * sum(CAPS)
        if h == 0:
            src = queue[k].at[pl.ds(d * CAPS[0], CAPS[0])]
        else:
            src = ring[k].at[pl.ds(base + starts[h - 1], CAPS[h])]
        return pltpu.make_async_remote_copy(
            src_ref=src,
            dst_ref=ring[k].at[pl.ds(base + starts[h], CAPS[h])],
            send_sem=z_send.at[k, d, h],
            recv_sem=z_recv.at[k, d, h],
            device_id=((up, down)[d], tensor),
            device_id_type=MESH,
        )

    def gather_copy(k, o):
        return pltpu.make_async_remote_copy(
            src_ref=gathered[k].at[pl.ds(peers[o] * each, each)],
            dst_ref=outs[k].at[me],
            send_sem=c_send.at[k, o],
            recv_sem=c_recv.at[k, o],
            device_id=partner[o],
            device_id_type=MESH,
        )

    def gather_self(k):
        return pltpu.make_async_copy(gathered[k].at[pl.ds(me * each, each)], outs[k].at[me], c_self.at[k])

    def begin(k):
        for o in range(1, RANKS):
            spread_copy(k, o).start()
        spread_self(k).start()

    def pack(k):
        for o in range(1, RANKS):
            spread_copy(k, o).wait_recv()
        spread_self(k).wait()

        @pl.loop(0, 2 * CAPS[0] // 8)
        def _(s):
            for u in range(8):
                at = s * 8 + u
                queue[k][at] = spread[k][send_tab[at]]

        for d in range(2):
            ring_copy(k, d, 0).start()

    def forward(k, h):
        for d in range(2):
            ring_copy(k, d, h - 1).wait_recv()
            ring_copy(k, d, h).start()

    def unpack(k):
        for d in range(2):
            ring_copy(k, d, 3).wait_recv()

        @pl.loop(0, width // 8)
        def _(s):
            for u in range(8):
                at = s * 8 + u
                gathered[k][at] = jnp.where(
                    flag_tab[at] == 1, spread[k][stay_tab[at]], ring[k][land_tab[at]]
                )

        for o in range(1, RANKS):
            gather_copy(k, o).start()
        gather_self(k).start()

    for k in range(count):
        begin(k)
    for step in range(count + 4):
        for stage in (4, 3, 2, 1, 0):
            k = step - stage
            if 0 <= k < count:
                if stage == 0:
                    pack(k)
                elif stage == 4:
                    unpack(k)
                else:
                    forward(k, stage)
    for k in range(count):
        for o in range(1, RANKS):
            gather_copy(k, o).wait_recv()
        gather_self(k).wait()
    for k in range(count):
        for o in range(1, RANKS):
            spread_copy(k, o).wait_send()
            gather_copy(k, o).wait_send()
        for d in range(2):
            for h in range(4):
                ring_copy(k, d, h).wait_send()


def migrate(tables, parts):
    count = len(parts)
    width = RANKS * parts[0].shape[1]
    smem = pl.BlockSpec(memory_space=pltpu.SMEM)
    anywhere = pl.BlockSpec(memory_space=pl.ANY)
    scratch = []
    for slots in (width, 2 * CAPS[0], 2 * sum(CAPS), width):
        for part in parts:
            scratch.append(pltpu.VMEM((slots,) + part.shape[2:], part.dtype))
    dma = pltpu.SemaphoreType.DMA
    scratch += [
        dma((count, RANKS)),
        dma((count, RANKS)),
        dma((count,)),
        dma((count, 2, 4)),
        dma((count, 2, 4)),
        dma((count, RANKS)),
        dma((count, RANKS)),
        dma((count,)),
    ]
    return pl.pallas_call(
        functools.partial(migrate_kernel, count),
        out_shape=[jax.ShapeDtypeStruct(part.shape, part.dtype) for part in parts],
        in_specs=[smem] * 4 + [anywhere] * count,
        out_specs=[anywhere] * count,
        scratch_shapes=scratch,
        compiler_params=pltpu.CompilerParams(
            collective_id=0, has_side_effects=True, vmem_limit_bytes=48 * 2**20
        ),
    )(*tables, *parts)


def cut(final_conv, final_state, key_rows, value_rows):
    requests, taps, channels = final_conv.shape
    states = final_state.shape[1]
    positions, width = key_rows.shape[1:]

    def cache(rows):
        split = rows.reshape(requests, positions // 16, 16, width // HEAD, HEAD)
        return split.transpose(3, 1, 0, 2, 4).reshape(-1, requests, 16, HEAD)

    conv = final_conv.reshape(requests, taps, RANKS, -1, HEAD).transpose(2, 0, 1, 3, 4)
    conv = conv.reshape(RANKS, requests, -1, HEAD)
    conv = jnp.pad(conv, ((0, 0), (0, 0), (0, 8 - conv.shape[2]), (0, 0)))
    state = final_state.reshape(requests, states, -1, RANKS, HEAD).transpose(2, 3, 0, 1, 4)
    return [jnp.concatenate([cache(key_rows), cache(value_rows)]), conv] + list(state)


def join(parts, shapes):
    caches, conv, *state = parts
    requests, taps, channels = shapes[0]
    positions, width = shapes[2][1:]

    def cache(rows):
        split = rows.reshape(width // HEAD, positions // 16, requests, 16, HEAD)
        return split.transpose(2, 1, 3, 0, 4).reshape(requests, positions, width)

    half = caches.shape[0] // 2
    pieces = channels // (RANKS * HEAD)
    conv = conv[:, :, : taps * pieces].reshape(RANKS, requests, taps, pieces, HEAD)
    conv = conv.transpose(1, 2, 0, 3, 4).reshape(shapes[0])
    state = jnp.stack(state).transpose(2, 3, 0, 1, 4).reshape(shapes[1])
    return conv, state, cache(caches[:half]), cache(caches[half:])


def slot_ranks(owners):
    slot_count = owners.shape[-1]
    slot_order = jnp.arange(slot_count, dtype=jnp.int32)
    earlier = slot_order[None, :] < slot_order[:, None]
    matching = owners[..., :, None] == owners[..., None, :]
    return jnp.sum(jnp.where(matching & earlier, 1, 0), axis=-1).astype(jnp.int32)


def pack_slots(values_in, send_slots, total_slots):
    return (
        jnp.zeros((total_slots,) + values_in.shape[1:], values_in.dtype)
        .at[send_slots]
        .set(values_in)
    )


def exchange(new_owner, arrays):
    requests_here = arrays[0].shape[0]
    sections = lax.axis_size("section")
    section_index = lax.axis_index("section")
    capacity = max(1, requests_here // sections)
    total_slots = sections * capacity
    owners = new_owner.reshape(sections, requests_here)
    my_owners = lax.dynamic_slice_in_dim(owners, section_index, 1, 0)[0]
    send_slots = my_owners * capacity + slot_ranks(my_owners)
    ranks_all = slot_ranks(owners)
    arriving = owners == section_index
    sources = jnp.arange(sections, dtype=jnp.int32)[:, None]
    recv_slots = jnp.sum(jnp.where(arriving, sources * capacity + ranks_all, 0), axis=0)
    def select(places, options, rows):
        chosen = (places[:, None] == jnp.arange(options)[None, :]).astype(rows.dtype)
        flat = rows.reshape(rows.shape[0], -1)
        picked = jnp.dot(chosen, flat, preferred_element_type=jnp.float32)
        return picked.astype(rows.dtype).reshape((places.shape[0],) + rows.shape[1:])

    return tuple(
        select(
            recv_slots,
            total_slots,
            lax.all_to_all(
                pack_slots(array, send_slots, total_slots),
                "section",
                split_axis=0,
                concat_axis=0,
                tiled=True,
            ),
        )
        for array in arrays
    )


def local(
    inner_input,
    gate_input,
    conv_state,
    mamba_state,
    conv_weight,
    conv_bias,
    xproj_weight,
    dt_gain,
    dtproj_weight,
    dt_bias,
    decay_rate,
    skip_gain,
    query,
    key_cache,
    value_cache,
    key_new,
    value_new,
    kv_length,
    new_owner,
):
    steps_count = inner_input.shape[0]
    requests_here = inner_input.shape[1]
    channels = inner_input.shape[2]
    tap_count = conv_weight.shape[0]
    rank_width = dt_gain.shape[0]
    state_width = mamba_state.shape[1]
    window = jnp.concatenate([conv_state, jnp.swapaxes(inner_input, 0, 1)], axis=1)
    conv_list = []
    for step_index in range(steps_count):
        summed = jnp.zeros((requests_here, channels), jnp.float32) + conv_bias
        for tap_index in range(tap_count):
            summed = summed + conv_weight[tap_index] * window[:, step_index + tap_index].astype(
                jnp.float32
            )
        conv_list.append(jax.nn.silu(summed).astype(jnp.bfloat16))
    conv_out = jnp.stack(conv_list)
    hidden = mamba_state.astype(jnp.float32)
    mamba_list = []
    for step_index in range(steps_count):
        projected = lax.psum(project_rows(conv_out[step_index], xproj_weight), "tensor")
        low_rank = projected[:, :rank_width]
        scaled = (
            low_rank
            * lax.rsqrt(jnp.mean(low_rank * low_rank, axis=-1, keepdims=True) + epsilon)
            * dt_gain
        ).astype(jnp.bfloat16)
        delta_rate = jax.nn.softplus(
            jnp.dot(scaled, dtproj_weight, preferred_element_type=jnp.float32) + dt_bias
        )
        input_gain = projected[:, rank_width : rank_width + state_width]
        output_gain = projected[:, rank_width + state_width :]
        inputs_now = conv_out[step_index].astype(jnp.float32)
        hidden = (
            jnp.exp(-delta_rate[:, None, :] * decay_rate[None]) * hidden
            + (delta_rate * inputs_now)[:, None, :] * input_gain[:, :, None]
        )
        reading = jnp.sum(hidden * output_gain[:, :, None], axis=1) + skip_gain * inputs_now
        mamba_list.append(
            (reading * jax.nn.silu(gate_input[step_index].astype(jnp.float32))).astype(jnp.bfloat16)
        )
    final_state = hidden.astype(jnp.bfloat16)
    final_conv = window[:, steps_count:]
    cache_slots = key_cache.shape[1]
    cache_heads = key_cache.shape[2] // HEAD
    query_heads = query.shape[2] // HEAD
    group_size = query_heads // cache_heads
    positions = jnp.arange(cache_slots, dtype=jnp.int32)
    key_rows = key_cache
    value_rows = value_cache
    attended = []
    for step_index in range(steps_count):
        target = kv_length + step_index
        written = (positions[None, :] == target[:, None])[:, :, None]
        key_rows = jnp.where(written, key_new[step_index][:, None, :], key_rows)
        value_rows = jnp.where(written, value_new[step_index][:, None, :], value_rows)
        queries = query[step_index].reshape(requests_here, cache_heads, group_size, HEAD)
        key_heads = key_rows.reshape(requests_here, cache_slots, cache_heads, HEAD)
        scores = jnp.einsum(
            "rgqd,rcgd->rgqc", queries, key_heads, preferred_element_type=jnp.float32
        ) / math.sqrt(HEAD)
        allowed = (positions[None, :] <= target[:, None])[:, None, None, :]
        scores = jnp.where(allowed, scores, -1e30)
        highest = jnp.max(scores, axis=-1, keepdims=True)
        weights = jnp.exp(scores - highest)
        weights = (weights / jnp.sum(weights, axis=-1, keepdims=True)).astype(jnp.bfloat16)
        value_heads = value_rows.reshape(requests_here, cache_slots, cache_heads, HEAD)
        mixed_out = jnp.einsum(
            "rgqc,rcgd->rgqd", weights, value_heads, preferred_element_type=jnp.float32
        )
        attended.append(mixed_out.reshape(requests_here, query_heads * HEAD).astype(jnp.bfloat16))
    arrays = (final_conv, final_state, key_rows, value_rows)
    fits, *tables = route_tables(new_owner, lax.axis_index("section") // RANKS)
    moved = lax.cond(
        fits,
        lambda: join(migrate(tables, cut(*arrays)), [a.shape for a in arrays]),
        lambda: exchange(new_owner, arrays),
    )
    return (jnp.stack(mamba_list), jnp.stack(attended), *moved)


def solution(mesh):
    in_specs = (
        P(None, "section", "tensor"),
        P(None, "section", "tensor"),
        P("section", None, "tensor"),
        P("section", None, "tensor"),
        P(None, "tensor"),
        P("tensor"),
        P(None, "tensor"),
        P(),
        P(None, "tensor"),
        P("tensor"),
        P(None, "tensor"),
        P("tensor"),
        P(None, "section", "tensor"),
        P("section", None, "tensor"),
        P("section", None, "tensor"),
        P(None, "section", "tensor"),
        P(None, "section", "tensor"),
        P("section"),
        P(),
    )
    out_specs = (
        P(None, "section", "tensor"),
        P(None, "section", "tensor"),
        P("section", None, "tensor"),
        P("section", None, "tensor"),
        P("section", None, "tensor"),
        P("section", None, "tensor"),
    )
    return jax.shard_map(local, mesh=mesh, in_specs=in_specs, out_specs=out_specs, check_vma=False)
```

```python
import functools
import math

import jax
import jax.numpy as jnp
from jax import lax
from jax.experimental import pallas as pl
from jax.experimental.pallas import tpu as pltpu
from jax.sharding import PartitionSpec as P

HEAD = 128
MESH = pl.DeviceIdType.MESH
PLANES = 8
RANKS = 8
CAPS = (120, 96, 68, 36)
STARTS = (0, CAPS[0], CAPS[0] + CAPS[1], CAPS[0] + CAPS[1] + CAPS[2])


epsilon = 1e-06


def table_kernel(owner_ref, out_ref, mem_ref):
    planes, width = owner_ref.shape
    each = width // RANKS
    plane = lax.axis_index("section") // RANKS
    owner = owner_ref[...]
    own_plane = lax.broadcasted_iota(jnp.int32, (planes, width), 0)
    packet = lax.broadcasted_iota(jnp.int32, (planes, width), 1)
    away = (owner // RANKS - own_plane + PLANES) % PLANES
    kind = jnp.where(away == 0, 7, jnp.where(away == 4, 0, jnp.where(away < 4, 4 - away, away - 1)))
    key = kind * width + packet
    key_columns = key.T
    rank = jnp.concatenate(
        [
            jnp.sum((key_columns[:, p : p + 1] < key[p : p + 1, :]).astype(jnp.int32), axis=0, keepdims=True)
            for p in range(planes)
        ]
    )
    count = [jnp.sum((kind == k).astype(jnp.int32), axis=1, keepdims=True) for k in range(7)]
    ties = count[0]
    ups = count[1] + count[2] + count[3]
    downs = count[4] + count[5] + count[6]
    ties_up = jnp.minimum(jnp.maximum((ups + ties + downs + 1) // 2 - ups, 0), ties)
    ties_down = ties - ties_up
    tied_up = rank < ties_up
    goes_up = jnp.where(kind == 0, tied_up.astype(jnp.int32), (kind <= 3).astype(jnp.int32))
    place = jnp.where(
        kind == 0,
        jnp.where(tied_up, rank, rank - ties_up),
        jnp.where(kind <= 3, rank - ties + ties_up, rank - ties - ups + ties_down),
    )
    hops = jnp.where(kind == 0, 4, jnp.where(kind <= 3, 4 - kind, 7 - kind))
    start = jnp.where(
        hops == 1, STARTS[0], jnp.where(hops == 2, STARTS[1], jnp.where(hops == 3, STARTS[2], STARTS[3]))
    )
    arrival = start + place + jnp.where(goes_up == 1, 0, sum(CAPS))
    over = jnp.zeros_like(ties)
    for ties_here, near in ((ties_up, count[1:4]), (ties_down, count[4:7])):
        load = ties_here
        for hop in (3, 2, 1, 0):
            over = over + (load > CAPS[hop]).astype(jnp.int32)
            if hop:
                load = load + near[3 - hop]
    over = jnp.sum(over, axis=0, keepdims=True)

    lane = jnp.where(kind == 7, -1, jnp.where(goes_up == 1, place, place + CAPS[0]))
    mem_ref[...] = jnp.where((goes_up == 1) & (place >= CAPS[0]), -1, lane)
    mine = jnp.broadcast_to(mem_ref[pl.ds(plane, 1), :], (8, width)).T[:, :1]
    slot = lax.broadcasted_iota(jnp.int32, (width, width), 1)
    number = lax.broadcasted_iota(jnp.int32, (width, width), 0)
    send = jnp.sum(jnp.where(mine == slot, number, 0), axis=0, keepdims=True)

    coded = jnp.where(kind == 7, packet + 65536, arrival)
    spot = lax.broadcasted_iota(jnp.int32, (1, width), 1) // each
    found = jnp.zeros((1, width), jnp.int32)
    for r in range(RANKS):
        row = jnp.sum(jnp.where(owner == plane * RANKS + r, coded, 0), axis=0, keepdims=True)
        shift = each
        while shift < width:
            row = row + pltpu.roll(row, shift, 1)
            shift *= 2
        found = jnp.where(spot == r, row, found)
    stays = found >= 65536
    out_ref[...] = jnp.concatenate(
        [
            send,
            jnp.where(stays, found - 65536, 0),
            jnp.where(stays, 0, found),
            stays.astype(jnp.int32),
            jnp.broadcast_to((over == 0).astype(jnp.int32), (4, width)),
        ]
    )


def route_tables(new_owner):
    width = new_owner.shape[0] // PLANES
    return pl.pallas_call(
        table_kernel,
        out_shape=jax.ShapeDtypeStruct((8, width), jnp.int32),
        in_specs=[pl.BlockSpec(memory_space=pltpu.VMEM)],
        out_specs=pl.BlockSpec(memory_space=pltpu.VMEM),
        scratch_shapes=[pltpu.VMEM((PLANES, width), jnp.int32)],
    )(new_owner.reshape(PLANES, width))


def silu(v):
    return v * (1.0 / (1.0 + jnp.exp(-v)))


LOADS = (
    "key_cache",
    "value_cache",
    "key_new",
    "value_new",
    "window",
    "conv_weight",
    "conv_bias",
    "xproj",
    "query",
    "lengths",
    "dt_gain",
    "dtproj",
    "dt_bias",
    "decay",
    "state",
    "gate",
    "skip",
)


def step_kernel(shapes, tab, kv_len, conv_in, *refs):
    total = len(LOADS)
    hbm = dict(zip(LOADS, refs[:total]))
    out_mamba, out_attn, out_conv, out_state, out_keys, out_values = refs[total : total + 6]
    rest = list(refs[total + 6 :])
    take = lambda n: [rest.pop(0) for _ in range(n)]
    mem = dict(zip(LOADS, take(total)))
    count = len(shapes)
    spread, queue, ring, gathered = take(count), take(count), take(count), take(count)
    caches, *states = take(count - 1)
    key_fresh, value_fresh, conv_out, low_parts, gain_parts, delta, push, reading, gains, mamba, attn = take(11)
    in_sem, a_send, a_recv, a_self, z_send, z_recv, c_send, c_recv, c_self, p_send, p_recv, o_sem = take(12)

    section = lax.axis_index("section")
    tensor = lax.axis_index("tensor")
    tensors = lax.axis_size("tensor")
    plane = section // RANKS
    me = section % RANKS
    width = spread[0].shape[0]
    each = width // RANKS
    up = lax.rem(plane + 1, PLANES) * RANKS + me
    down = lax.rem(plane + PLANES - 1, PLANES) * RANKS + me
    peers = [lax.rem(me + o, RANKS) for o in range(RANKS)]
    partner = [(plane * RANKS + p, tensor) for p in peers]
    beside = [(section, lax.rem(tensor + o, tensors)) for o in range(tensors)]

    def load(name):
        return pltpu.make_async_copy(hbm[name], mem[name], in_sem.at[LOADS.index(name)])

    for name in LOADS:
        load(name).start()

    barrier = pltpu.get_barrier_semaphore()
    friends = partner[1:] + [(up, tensor), (down, tensor)] + beside[1:]
    for device in friends:
        pl.semaphore_signal(barrier, inc=1, device_id=device, device_id_type=MESH)
    pl.semaphore_wait(barrier, len(friends))

    def lanes(at, size):
        return pl.ds(pl.multiple_of(at, HEAD), size)

    def part(k, rank):
        if k == 0:
            return conv_in.at[:, :, lanes(rank * 2 * HEAD, 2 * HEAD)]
        return (caches if k == 1 else states[k - 2]).at[rank]

    def spread_copy(k, o):
        return pltpu.make_async_remote_copy(
            src_ref=part(k, peers[o]),
            dst_ref=spread[k].at[pl.ds(me * each, each)],
            send_sem=a_send.at[k, o],
            recv_sem=a_recv.at[k, o],
            device_id=partner[o],
            device_id_type=MESH,
        )

    def spread_self(k):
        return pltpu.make_async_copy(part(k, me), spread[k].at[pl.ds(me * each, each)], a_self.at[k])

    def ring_copy(k, d, h):
        base = d * sum(CAPS)
        if h == 0:
            src = queue[k].at[pl.ds(d * CAPS[0], CAPS[0])]
        else:
            src = ring[k].at[pl.ds(base + STARTS[h - 1], CAPS[h])]
        return pltpu.make_async_remote_copy(
            src_ref=src,
            dst_ref=ring[k].at[pl.ds(base + STARTS[h], CAPS[h])],
            send_sem=z_send.at[k, d, h],
            recv_sem=z_recv.at[k, d, h],
            device_id=((up, down)[d], tensor),
            device_id_type=MESH,
        )

    def home(k, values):
        if k == 0:
            return out_conv.at[:, :, lanes(me * 2 * HEAD, 2 * HEAD)]
        if k == 1:
            at = lax.rem(me, 4)
            rows = pl.ds(pl.multiple_of(lax.rem(at, 2) * 16, 16), 16)
            return (out_values if values else out_keys).at[:, rows, lanes(at // 2 * HEAD, HEAD)]
        return out_state.at[:, :, lanes((k - 2) * RANKS * HEAD + me * HEAD, HEAD)]

    def gather_copy(k, o, values=False):
        return pltpu.make_async_remote_copy(
            src_ref=gathered[k].at[pl.ds(peers[o] * each, each)],
            dst_ref=home(k, values),
            send_sem=c_send.at[k, o],
            recv_sem=c_recv.at[k, o],
            device_id=partner[o],
            device_id_type=MESH,
        )

    def gather_self(k, values=False):
        return pltpu.make_async_copy(
            gathered[k].at[pl.ds(me * each, each)], home(k, values), c_self.at[k]
        )

    def begin(k):
        for o in range(1, RANKS):
            spread_copy(k, o).start()
        spread_self(k).start()

    def pack(k):
        for o in range(1, RANKS):
            spread_copy(k, o).wait_recv()
        spread_self(k).wait()

        @pl.loop(0, 2 * CAPS[0] // 8)
        def _(s):
            for u in range(8):
                at = s * 8 + u
                queue[k][at] = spread[k][tab[0, at]]

        for d in range(2):
            ring_copy(k, d, 0).start()

    def forward(k, h):
        for d in range(2):
            ring_copy(k, d, h - 1).wait_recv()
            ring_copy(k, d, h).start()

    def unpack(k):
        for d in range(2):
            ring_copy(k, d, 3).wait_recv()

        @pl.loop(0, width // 8)
        def _(s):
            for u in range(8):
                at = s * 8 + u
                gathered[k][at] = jnp.where(
                    tab[3, at] == 1, spread[k][tab[1, at]], ring[k][tab[2, at]]
                )

        def send(values):
            for o in range(1, RANKS):
                gather_copy(k, o, values).start()
            gather_self(k, values).start()

        if k == 1:
            pl.when(me < 4)(lambda: send(False))
            pl.when(me >= 4)(lambda: send(True))
        else:
            send(False)

    requests = each
    channels = conv_out.shape[1]
    steps = conv_out.shape[0] // requests

    def update_caches():
        load("key_new").wait()
        load("value_new").wait()
        key_fresh[...] = mem["key_new"][...].astype(jnp.float32)
        value_fresh[...] = mem["value_new"][...].astype(jnp.float32)
        load("key_cache").wait()
        load("value_cache").wait()

        @pl.loop(0, requests // 8)
        def _(block):
            ats = [pl.ds(pl.multiple_of(s * requests + block * 8, 8), 8) for s in range(steps)]
            for base, cache, fresh in ((0, mem["key_cache"], key_fresh), (4, mem["value_cache"], value_fresh)):
                for g in range(2):
                    cols = slice(g * HEAD, (g + 1) * HEAD)
                    new = [fresh[at, cols] for at in ats]
                    for u in range(8):
                        r = block * 8 + u
                        for p in range(2):
                            rows = lax.broadcasted_iota(jnp.int32, (16, HEAD), 0) + p * 16
                            tile = cache[r, p * 16 : p * 16 + 16, cols].astype(jnp.float32)
                            for s in range(steps):
                                tile = jnp.where(rows == kv_len[r] + s, new[s][u : u + 1], tile)
                            caches[base + g * 2 + p, r] = tile.astype(caches.dtype)

    def convolve():
        load("window").wait()
        load("conv_weight").wait()
        load("conv_bias").wait()
        taps = mem["conv_weight"].shape[0]

        @pl.loop(0, channels // 256)
        def _(b):
            cols = pl.ds(pl.multiple_of(b * 256, 256), 256)
            for s in range(steps):
                total_in = mem["conv_bias"][:, cols]
                for k in range(taps):
                    total_in = total_in + mem["conv_weight"][k : k + 1, cols] * mem["window"][
                        s + k, :, cols
                    ].astype(jnp.float32)
                conv_out[s * requests : (s + 1) * requests, cols] = silu(total_in).astype(conv_out.dtype)

    def share_copies(o):
        return [
            pltpu.make_async_remote_copy(
                src_ref=buf.at[tensor],
                dst_ref=buf.at[tensor],
                send_sem=p_send.at[n, o],
                recv_sem=p_recv.at[n, o],
                device_id=beside[o],
                device_id_type=MESH,
            )
            for n, buf in enumerate((low_parts, gain_parts))
        ]

    rank_width = low_parts.shape[2]
    state_width = gains.shape[1] // 2
    nt = (((1,), (1,)), ((), ()))

    def project():
        load("xproj").wait()
        low_parts[tensor] = lax.dot_general(
            conv_out[...], mem["xproj"][:rank_width], nt, preferred_element_type=jnp.float32
        )
        gain_parts[tensor, :, : steps * requests] = lax.dot_general(
            mem["xproj"][rank_width:], conv_out[...], nt, preferred_element_type=jnp.float32
        )
        for o in range(1, tensors):
            for copy in share_copies(o):
                copy.start()

    def rates():
        for o in range(1, tensors):
            for copy in share_copies(o):
                copy.wait_recv()
        low = low_parts[0]
        both = gain_parts[0]
        for t in range(1, tensors):
            low = low + low_parts[t]
            both = both + gain_parts[t]
        load("dt_gain").wait()
        load("dtproj").wait()
        load("dt_bias").wait()
        mean = jnp.mean(low * low, axis=-1, keepdims=True)
        scaled = (low * lax.rsqrt(mean + epsilon) * mem["dt_gain"][...]).astype(conv_out.dtype)
        for b in range(channels // 512):
            cols = slice(b * 512, (b + 1) * 512)
            rate = (
                jnp.dot(scaled, mem["dtproj"][:, cols], preferred_element_type=jnp.float32)
                + mem["dt_bias"][:, cols]
            )
            rate = jnp.maximum(rate, 0.0) + jnp.log1p(jnp.exp(-jnp.abs(rate)))
            delta[:, cols] = rate
            push[:, cols] = rate * conv_out[:, cols].astype(jnp.float32)
        for c in range(steps * requests):
            gains[c] = jnp.broadcast_to(both[:, c : c + 1], (2 * state_width, HEAD))

    def recur(half):
        @pl.loop(0, requests // 8 * 4)
        def _(turn):
            block, b = turn // 4, lax.rem(turn, 4)
            cols = pl.ds(pl.multiple_of(half * RANKS * HEAD + b * 256, 256), 256)
            ats = [pl.ds(pl.multiple_of(s * requests + block * 8, 8), 8) for s in range(steps)]
            decay = mem["decay"][:, cols]
            rates_now = [delta[at, cols] for at in ats]
            push_now = [push[at, cols] for at in ats]
            read = [[] for _ in ats]
            for u in range(8):
                r = block * 8 + u
                hidden = mem["state"][r, :, cols].astype(jnp.float32)
                for s in range(steps):
                    gain_in = gains[s * requests + r, :state_width]
                    gain_out = gains[s * requests + r, state_width:]
                    gain_in = jnp.concatenate([gain_in, gain_in], axis=1)
                    gain_out = jnp.concatenate([gain_out, gain_out], axis=1)
                    hidden = (
                        jnp.exp(-rates_now[s][u : u + 1] * decay) * hidden
                        + push_now[s][u : u + 1] * gain_in
                    )
                    read[s].append(jnp.sum(hidden * gain_out, axis=0, keepdims=True))
                final = hidden.astype(states[half].dtype)
                states[half][2 * b, r] = final[:, :HEAD]
                states[half][2 * b + 1, r] = final[:, HEAD:]
            for s in range(steps):
                reading[ats[s], cols] = jnp.concatenate(read[s])

    def gate():
        load("gate").wait()
        load("skip").wait()

        @pl.loop(0, channels // 256)
        def _(b):
            cols = pl.ds(pl.multiple_of(b * 256, 256), 256)
            for s in range(steps):
                rows = slice(s * requests, (s + 1) * requests)
                read = reading[rows, cols] + mem["skip"][:, cols] * conv_out[rows, cols].astype(jnp.float32)
                mamba[s, :, cols] = (read * silu(mem["gate"][s, :, cols].astype(jnp.float32))).astype(mamba.dtype)

        pltpu.make_async_copy(mamba, out_mamba, o_sem.at[0]).start()

    group = mem["query"].shape[2] // HEAD // 2

    def attend(half, g):
        rows16 = slice(half * 16, half * 16 + 16)
        query = jnp.concatenate(
            [
                mem["query"][s, rows16, (g * group + h) * HEAD : (g * group + h + 1) * HEAD]
                for s in range(steps)
                for h in range(group)
            ]
        )
        size = query.shape[0]
        row = lax.broadcasted_iota(jnp.int32, (size, 256), 0)
        col = lax.broadcasted_iota(jnp.int32, (size, 256), 1)
        limit = mem["lengths"][half : half + 1, :] + row // (size // steps)
        scores = []
        for p in range(2):
            keys = caches[g * 2 + p, rows16].reshape(256, HEAD)
            score = lax.dot_general(query, keys, nt, preferred_element_type=jnp.float32) / math.sqrt(HEAD)
            allowed = (row % 16 == col // 16) & (col % 16 + p * 16 <= limit)
            scores.append(jnp.where(allowed, score, -1e30))
        highest = jnp.maximum(
            jnp.max(scores[0], axis=-1, keepdims=True), jnp.max(scores[1], axis=-1, keepdims=True)
        )
        weights = [jnp.exp(score - highest) for score in scores]
        whole = jnp.sum(weights[0], axis=-1, keepdims=True) + jnp.sum(weights[1], axis=-1, keepdims=True)
        inverse = 1.0 / whole
        mixed = jnp.zeros((size, HEAD), jnp.float32)
        for p in range(2):
            values = caches[4 + g * 2 + p, rows16].reshape(256, HEAD)
            mixed = mixed + jnp.dot(
                (weights[p] * inverse).astype(values.dtype), values, preferred_element_type=jnp.float32
            )
        mixed = mixed.astype(attn.dtype)
        for s in range(steps):
            for h in range(group):
                at = (s * group + h) * 16
                attn[s, rows16, (g * group + h) * HEAD : (g * group + h + 1) * HEAD] = mixed[at : at + 16]

    begin(0)
    update_caches()
    begin(1)
    convolve()
    project()
    pack(0)
    load("query").wait()
    load("lengths").wait()
    for half in range(2):
        attend(half, 0)
    pack(1)
    load("decay").wait()
    load("state").wait()
    rates()
    recur(0)
    begin(2)
    forward(0, 1)
    recur(1)
    begin(3)
    forward(1, 1)
    forward(0, 2)
    for half in range(2):
        attend(half, 1)
    pltpu.make_async_copy(attn, out_attn, o_sem.at[1]).start()
    pack(2)
    gate()
    forward(1, 2)
    forward(0, 3)
    pack(3)
    forward(2, 1)
    forward(1, 3)
    unpack(0)
    forward(3, 1)
    forward(2, 2)
    unpack(1)
    forward(3, 2)
    forward(2, 3)
    forward(3, 3)
    unpack(2)
    unpack(3)

    for k in range(count):
        for o in range(1, RANKS):
            gather_copy(k, o).wait_recv()
        gather_self(k).wait()
    pltpu.make_async_copy(mamba, out_mamba, o_sem.at[0]).wait()
    pltpu.make_async_copy(attn, out_attn, o_sem.at[1]).wait()
    for k in range(count):
        for o in range(1, RANKS):
            spread_copy(k, o).wait_send()
            gather_copy(k, o).wait_send()
        for d in range(2):
            for h in range(4):
                ring_copy(k, d, h).wait_send()
    for o in range(1, tensors):
        for copy in share_copies(o):
            copy.wait_send()


def fast_steps(tables, kv_length, final_conv, loads, outs):
    requests, _, channels = final_conv.shape
    steps = loads["query"].shape[0]
    width = RANKS * requests
    kind = final_conv.dtype
    slices = [(final_conv.shape[1], 2 * HEAD), (16, HEAD), (16, HEAD), (16, HEAD)]
    count = len(slices)
    rank_width = loads["dtproj"].shape[0]
    gains = loads["xproj"].shape[0] - rank_width
    rows = steps * requests
    tensors = lax.axis_size("tensor")
    smem = pl.BlockSpec(memory_space=pltpu.SMEM)
    anywhere = pl.BlockSpec(memory_space=pl.ANY)
    f32 = jnp.float32
    scratch = [pltpu.VMEM(loads[name].shape, loads[name].dtype) for name in LOADS]
    for slots in (width, 2 * CAPS[0], 2 * sum(CAPS), width):
        scratch += [pltpu.VMEM((slots,) + each, kind) for each in slices]
    scratch += [pltpu.VMEM((RANKS, requests) + each, kind) for each in slices[1:]]
    scratch += [
        pltpu.VMEM(loads["key_new"].shape, f32),
        pltpu.VMEM(loads["value_new"].shape, f32),
        pltpu.VMEM((rows, channels), kind),
        pltpu.VMEM((tensors, rows, rank_width), f32),
        pltpu.VMEM((tensors, gains, HEAD), f32),
        pltpu.VMEM((rows, channels), f32),
        pltpu.VMEM((rows, channels), f32),
        pltpu.VMEM((rows, channels), f32),
        pltpu.VMEM((rows, gains, HEAD), f32),
        pltpu.VMEM((steps, requests, channels), kind),
        pltpu.VMEM((steps, requests, channels), kind),
    ]
    dma = pltpu.SemaphoreType.DMA
    scratch += [
        dma((len(LOADS),)),
        dma((count, RANKS)),
        dma((count, RANKS)),
        dma((count,)),
        dma((count, 2, 4)),
        dma((count, 2, 4)),
        dma((count, RANKS)),
        dma((count, RANKS)),
        dma((count,)),
        dma((2, tensors)),
        dma((2, tensors)),
        dma((2,)),
    ]
    return pl.pallas_call(
        functools.partial(step_kernel, slices),
        out_shape=[jax.ShapeDtypeStruct(shape, kind) for shape in outs],
        in_specs=[smem, smem] + [anywhere] * (1 + len(LOADS)),
        out_specs=[anywhere] * 6,
        scratch_shapes=scratch,
        compiler_params=pltpu.CompilerParams(
            collective_id=0, has_side_effects=True, vmem_limit_bytes=56 * 2**20
        ),
    )(tables, kv_length, final_conv, *[loads[name] for name in LOADS])


def project_rows(conv_rows, xproj_weight):
    return lax.dot_general(
        conv_rows, xproj_weight, (((1,), (1,)), ((), ())), preferred_element_type=jnp.float32
    )


def slot_ranks(owners):
    slot_count = owners.shape[-1]
    slot_order = jnp.arange(slot_count, dtype=jnp.int32)
    earlier = slot_order[None, :] < slot_order[:, None]
    matching = owners[..., :, None] == owners[..., None, :]
    return jnp.sum(jnp.where(matching & earlier, 1, 0), axis=-1).astype(jnp.int32)


def pack_slots(values_in, send_slots, total_slots):
    return (
        jnp.zeros((total_slots,) + values_in.shape[1:], values_in.dtype)
        .at[send_slots]
        .set(values_in)
    )


def exchange(new_owner, arrays):
    requests_here = arrays[0].shape[0]
    sections = lax.axis_size("section")
    section_index = lax.axis_index("section")
    capacity = max(1, requests_here // sections)
    total_slots = sections * capacity
    owners = new_owner.reshape(sections, requests_here)
    my_owners = lax.dynamic_slice_in_dim(owners, section_index, 1, 0)[0]
    send_slots = my_owners * capacity + slot_ranks(my_owners)
    ranks_all = slot_ranks(owners)
    arriving = owners == section_index
    sources = jnp.arange(sections, dtype=jnp.int32)[:, None]
    recv_slots = jnp.sum(jnp.where(arriving, sources * capacity + ranks_all, 0), axis=0)
    def select(places, options, rows):
        chosen = (places[:, None] == jnp.arange(options)[None, :]).astype(rows.dtype)
        flat = rows.reshape(rows.shape[0], -1)
        picked = jnp.dot(chosen, flat, preferred_element_type=jnp.float32)
        return picked.astype(rows.dtype).reshape((places.shape[0],) + rows.shape[1:])

    return tuple(
        select(
            recv_slots,
            total_slots,
            lax.all_to_all(
                pack_slots(array, send_slots, total_slots),
                "section",
                split_axis=0,
                concat_axis=0,
                tiled=True,
            ),
        )
        for array in arrays
    )


def plain_steps(
    inner_input,
    gate_input,
    conv_state,
    mamba_state,
    conv_weight,
    conv_bias,
    xproj_weight,
    dt_gain,
    dtproj_weight,
    dt_bias,
    decay_rate,
    skip_gain,
    query,
    key_cache,
    value_cache,
    key_new,
    value_new,
    kv_length,
    new_owner,
):
    steps_count = inner_input.shape[0]
    requests_here = inner_input.shape[1]
    channels = inner_input.shape[2]
    tap_count = conv_weight.shape[0]
    rank_width = dt_gain.shape[0]
    state_width = mamba_state.shape[1]
    window = jnp.concatenate([conv_state, jnp.swapaxes(inner_input, 0, 1)], axis=1)
    conv_list = []
    for step_index in range(steps_count):
        summed = jnp.zeros((requests_here, channels), jnp.float32) + conv_bias
        for tap_index in range(tap_count):
            summed = summed + conv_weight[tap_index] * window[:, step_index + tap_index].astype(
                jnp.float32
            )
        conv_list.append(jax.nn.silu(summed).astype(jnp.bfloat16))
    conv_out = jnp.stack(conv_list)
    hidden = mamba_state.astype(jnp.float32)
    mamba_list = []
    for step_index in range(steps_count):
        projected = lax.psum(project_rows(conv_out[step_index], xproj_weight), "tensor")
        low_rank = projected[:, :rank_width]
        scaled = (
            low_rank
            * lax.rsqrt(jnp.mean(low_rank * low_rank, axis=-1, keepdims=True) + epsilon)
            * dt_gain
        ).astype(jnp.bfloat16)
        delta_rate = jax.nn.softplus(
            jnp.dot(scaled, dtproj_weight, preferred_element_type=jnp.float32) + dt_bias
        )
        input_gain = projected[:, rank_width : rank_width + state_width]
        output_gain = projected[:, rank_width + state_width :]
        inputs_now = conv_out[step_index].astype(jnp.float32)
        hidden = (
            jnp.exp(-delta_rate[:, None, :] * decay_rate[None]) * hidden
            + (delta_rate * inputs_now)[:, None, :] * input_gain[:, :, None]
        )
        reading = jnp.sum(hidden * output_gain[:, :, None], axis=1) + skip_gain * inputs_now
        mamba_list.append(
            (reading * jax.nn.silu(gate_input[step_index].astype(jnp.float32))).astype(jnp.bfloat16)
        )
    final_state = hidden.astype(jnp.bfloat16)
    final_conv = window[:, steps_count:]
    cache_slots = key_cache.shape[1]
    cache_heads = key_cache.shape[2] // HEAD
    query_heads = query.shape[2] // HEAD
    group_size = query_heads // cache_heads
    positions = jnp.arange(cache_slots, dtype=jnp.int32)
    key_rows = key_cache
    value_rows = value_cache
    attended = []
    for step_index in range(steps_count):
        target = kv_length + step_index
        written = (positions[None, :] == target[:, None])[:, :, None]
        key_rows = jnp.where(written, key_new[step_index][:, None, :], key_rows)
        value_rows = jnp.where(written, value_new[step_index][:, None, :], value_rows)
        queries = query[step_index].reshape(requests_here, cache_heads, group_size, HEAD)
        key_heads = key_rows.reshape(requests_here, cache_slots, cache_heads, HEAD)
        scores = jnp.einsum(
            "rgqd,rcgd->rgqc", queries, key_heads, preferred_element_type=jnp.float32
        ) / math.sqrt(HEAD)
        allowed = (positions[None, :] <= target[:, None])[:, None, None, :]
        scores = jnp.where(allowed, scores, -1e30)
        highest = jnp.max(scores, axis=-1, keepdims=True)
        weights = jnp.exp(scores - highest)
        weights = (weights / jnp.sum(weights, axis=-1, keepdims=True)).astype(jnp.bfloat16)
        value_heads = value_rows.reshape(requests_here, cache_slots, cache_heads, HEAD)
        mixed_out = jnp.einsum(
            "rgqc,rcgd->rgqd", weights, value_heads, preferred_element_type=jnp.float32
        )
        attended.append(mixed_out.reshape(requests_here, query_heads * HEAD).astype(jnp.bfloat16))
    arrays = (final_conv, final_state, key_rows, value_rows)
    moved = exchange(new_owner, arrays)
    return (jnp.stack(mamba_list), jnp.stack(attended), *moved)


def local(
    inner_input,
    gate_input,
    conv_state,
    mamba_state,
    conv_weight,
    conv_bias,
    xproj_weight,
    dt_gain,
    dtproj_weight,
    dt_bias,
    decay_rate,
    skip_gain,
    query,
    key_cache,
    value_cache,
    key_new,
    value_new,
    kv_length,
    new_owner,
):
    steps, requests, channels = inner_input.shape
    positions, width = key_cache.shape[1:]
    tables = route_tables(new_owner)
    final_conv = jnp.concatenate([conv_state[:, steps:], jnp.swapaxes(inner_input, 0, 1)], axis=1)
    loads = {
        "key_cache": key_cache,
        "value_cache": value_cache,
        "key_new": key_new.reshape(steps * requests, width),
        "value_new": value_new.reshape(steps * requests, width),
        "window": jnp.concatenate([jnp.swapaxes(conv_state, 0, 1), inner_input]),
        "conv_weight": conv_weight,
        "conv_bias": conv_bias.reshape(1, channels),
        "xproj": xproj_weight,
        "query": query,
        "lengths": jnp.repeat(kv_length.reshape(2, requests // 2), 16, axis=1),
        "dt_gain": dt_gain.reshape(1, -1),
        "dtproj": dtproj_weight,
        "dt_bias": dt_bias.reshape(1, channels),
        "decay": decay_rate,
        "state": mamba_state,
        "gate": gate_input,
        "skip": skip_gain.reshape(1, channels),
    }
    outs = [
        inner_input.shape,
        query.shape,
        conv_state.shape,
        mamba_state.shape,
        key_cache.shape,
        value_cache.shape,
    ]
    return lax.cond(
        tables[4, 0] == 1,
        lambda: tuple(fast_steps(tables, kv_length, final_conv, loads, outs)),
        lambda: plain_steps(
            inner_input,
            gate_input,
            conv_state,
            mamba_state,
            conv_weight,
            conv_bias,
            xproj_weight,
            dt_gain,
            dtproj_weight,
            dt_bias,
            decay_rate,
            skip_gain,
            query,
            key_cache,
            value_cache,
            key_new,
            value_new,
            kv_length,
            new_owner,
        ),
    )


def solution(mesh):
    in_specs = (
        P(None, "section", "tensor"),
        P(None, "section", "tensor"),
        P("section", None, "tensor"),
        P("section", None, "tensor"),
        P(None, "tensor"),
        P("tensor"),
        P(None, "tensor"),
        P(),
        P(None, "tensor"),
        P("tensor"),
        P(None, "tensor"),
        P("tensor"),
        P(None, "section", "tensor"),
        P("section", None, "tensor"),
        P("section", None, "tensor"),
        P(None, "section", "tensor"),
        P(None, "section", "tensor"),
        P("section"),
        P(),
    )
    out_specs = (
        P(None, "section", "tensor"),
        P(None, "section", "tensor"),
        P("section", None, "tensor"),
        P("section", None, "tensor"),
        P("section", None, "tensor"),
        P("section", None, "tensor"),
    )
    return jax.shard_map(local, mesh=mesh, in_specs=in_specs, out_specs=out_specs, check_vma=False)
```

```python
import functools
import math

import jax
import jax.numpy as jnp
from jax import lax
from jax.experimental import pallas as pl
from jax.experimental.pallas import tpu as pltpu
from jax.sharding import PartitionSpec as P

HEAD = 128
MESH = pl.DeviceIdType.MESH
PLANES = 8
RANKS = 8
TIGHT = (118, 86, 54, 22)
CAPS = (124, 94, 62, 30)
STARTS = (0, CAPS[0], CAPS[0] + CAPS[1], CAPS[0] + CAPS[1] + CAPS[2])


epsilon = 1e-06


def table_kernel(owner_ref, out_ref, mem_ref):
    planes, width = mem_ref.shape
    each = width // RANKS
    plane = lax.axis_index("section") // RANKS
    step = width // HEAD
    owner = jnp.concatenate([owner_ref[pl.ds(n, planes, stride=step), :] for n in range(step)], axis=1)
    own_plane = lax.broadcasted_iota(jnp.int32, (planes, width), 0)
    packet = lax.broadcasted_iota(jnp.int32, (planes, width), 1)
    away = (owner // RANKS - own_plane + PLANES) % PLANES
    kind = jnp.where(away == 0, 7, jnp.where(away == 4, 0, jnp.where(away < 4, 4 - away, away - 1)))
    key = kind * width + packet
    key_columns = key.T
    rank = jnp.concatenate(
        [
            jnp.sum((key_columns[:, p : p + 1] < key[p : p + 1, :]).astype(jnp.int32), axis=0, keepdims=True)
            for p in range(planes)
        ]
    )
    count = [jnp.sum((kind == k).astype(jnp.int32), axis=1, keepdims=True) for k in range(7)]
    ties = count[0]
    ups = count[1] + count[2] + count[3]
    downs = count[4] + count[5] + count[6]
    even = jnp.minimum(jnp.maximum((ups + ties + downs + 1) // 2 - ups, 0), ties)

    def share(caps):
        room = []
        for near in (count[1:4], count[4:7]):
            left = jnp.minimum(ties, caps[3] - near[0] * 0)
            load = near[0]
            for hop in (2, 1, 0):
                left = jnp.minimum(left, caps[hop] - load)
                if hop:
                    load = load + near[3 - hop]
            room.append(left)
        bad = (room[0] < 0) | (room[1] < 0) | (room[0] + room[1] < ties)
        chosen = jnp.minimum(jnp.maximum(even, ties - room[1]), room[0])
        return chosen, jnp.sum(bad.astype(jnp.int32), axis=0, keepdims=True)

    tight_up, tight_bad = share(TIGHT)
    loose_up, loose_bad = share(CAPS)
    ties_up = jnp.where(tight_bad == 0, tight_up, loose_up)
    level = jnp.where(tight_bad == 0, 0, jnp.where(loose_bad == 0, 1, 2))
    ties_down = ties - ties_up
    tied_up = rank < ties_up
    goes_up = jnp.where(kind == 0, tied_up.astype(jnp.int32), (kind <= 3).astype(jnp.int32))
    place = jnp.where(
        kind == 0,
        jnp.where(tied_up, rank, rank - ties_up),
        jnp.where(kind <= 3, rank - ties + ties_up, rank - ties - ups + ties_down),
    )
    hops = jnp.where(kind == 0, 4, jnp.where(kind <= 3, 4 - kind, 7 - kind))
    start = jnp.where(
        hops == 1, STARTS[0], jnp.where(hops == 2, STARTS[1], jnp.where(hops == 3, STARTS[2], STARTS[3]))
    )
    arrival = start + place + jnp.where(goes_up == 1, 0, sum(CAPS))
    lane = jnp.where(kind == 7, -1, jnp.where(goes_up == 1, place, place + CAPS[0]))
    mem_ref[...] = jnp.where((goes_up == 1) & (place >= CAPS[0]), -1, lane)
    mine = jnp.broadcast_to(mem_ref[pl.ds(plane, 1), :], (8, width)).T[:, :1]
    slot = lax.broadcasted_iota(jnp.int32, (width, width), 1)
    number = lax.broadcasted_iota(jnp.int32, (width, width), 0)
    send = jnp.sum(jnp.where(mine == slot, number, 0), axis=0, keepdims=True)

    coded = jnp.where(kind == 7, packet + 65536, arrival)
    spot = lax.broadcasted_iota(jnp.int32, (1, width), 1) // each
    found = jnp.zeros((1, width), jnp.int32)
    for r in range(RANKS):
        row = jnp.sum(jnp.where(owner == plane * RANKS + r, coded, 0), axis=0, keepdims=True)
        shift = each
        while shift < width:
            row = row + pltpu.roll(row, shift, 1)
            shift *= 2
        found = jnp.where(spot == r, row, found)
    stays = found >= 65536
    out_ref[...] = jnp.concatenate(
        [
            send,
            jnp.where(stays, found - 65536, 0),
            jnp.where(stays, 0, found),
            stays.astype(jnp.int32),
            jnp.broadcast_to(level, (4, width)),
        ]
    )


def route_tables(new_owner):
    width = new_owner.shape[0] // PLANES
    return pl.pallas_call(
        table_kernel,
        out_shape=jax.ShapeDtypeStruct((8, width), jnp.int32),
        in_specs=[pl.BlockSpec(memory_space=pltpu.VMEM)],
        out_specs=pl.BlockSpec(memory_space=pltpu.VMEM),
        scratch_shapes=[pltpu.VMEM((PLANES, width), jnp.int32)],
    )(new_owner.reshape(-1, HEAD))


def silu(v):
    return v * (1.0 / (1.0 + jnp.exp(-v)))


LOADS = (
    "key_cache",
    "value_cache",
    "key_new",
    "value_new",
    "old",
    "fresh",
    "conv_weight",
    "conv_bias",
    "xproj",
    "query",
    "dt_gain",
    "dtproj",
    "dt_bias",
    "decay",
    "state",
    "gate",
    "skip",
)


def step_kernel(count, caps, tab, kv_len, *refs):
    total = len(LOADS)
    hbm = dict(zip(LOADS, refs[:total]))
    out_mamba, out_attn, out_conv, out_state, out_keys, out_values = refs[total : total + 6]
    rest = list(refs[total + 6 :])
    take = lambda n: [rest.pop(0) for _ in range(n)]
    mem = dict(zip(LOADS, take(total)))
    spread, queue, ring, gathered, staged = take(count), take(count), take(count), take(count), take(count)
    caches, loose, *conv_landed = take(4)
    conv_final, lengths = take(2)
    key_fresh, value_fresh, conv_out, low_parts, gain_parts, delta, push, reading, gains, mamba, attn = take(11)
    flat = take(4)
    in_sem, a_send, a_recv, a_self, z_send, z_recv, c_send, c_recv, c_self, p_send, p_recv, o_sem = take(12)

    section = lax.axis_index("section")
    tensor = lax.axis_index("tensor")
    tensors = lax.axis_size("tensor")
    plane = section // RANKS
    me = section % RANKS
    width = spread[0].shape[0]
    each = width // RANKS
    up = lax.rem(plane + 1, PLANES) * RANKS + me
    down = lax.rem(plane + PLANES - 1, PLANES) * RANKS + me
    peers = [lax.rem(me + o, RANKS) for o in range(RANKS)]
    partner = [(plane * RANKS + p, tensor) for p in peers]
    beside = [(section, lax.rem(tensor + o, tensors)) for o in range(tensors)]

    def load(name):
        return pltpu.make_async_copy(hbm[name], mem[name], in_sem.at[LOADS.index(name)])

    for name in LOADS:
        load(name).start()

    barrier = pltpu.get_barrier_semaphore()
    friends = partner[1:] + [(up, tensor), (down, tensor)] + beside[1:]
    for device in friends:
        pl.semaphore_signal(barrier, inc=1, device_id=device, device_id_type=MESH)

    def lanes(at, size):
        return pl.ds(pl.multiple_of(at, HEAD), size)

    def part(k, rank):
        return staged[k].at[rank]

    def spread_copy(k, o):
        return pltpu.make_async_remote_copy(
            src_ref=part(k, peers[o]),
            dst_ref=spread[k].at[pl.ds(me * each, each)],
            send_sem=a_send.at[k, o],
            recv_sem=a_recv.at[k, o],
            device_id=partner[o],
            device_id_type=MESH,
        )

    def spread_self(k):
        return pltpu.make_async_copy(part(k, me), spread[k].at[pl.ds(me * each, each)], a_self.at[k])

    def ring_copy(k, d, h):
        base = d * sum(CAPS)
        if h == 0:
            src = queue[k].at[pl.ds(d * CAPS[0], caps[0])]
        else:
            src = ring[k].at[pl.ds(base + STARTS[h - 1], caps[h])]
        return pltpu.make_async_remote_copy(
            src_ref=src,
            dst_ref=ring[k].at[pl.ds(base + STARTS[h], caps[h])],
            send_sem=z_send.at[k, d, h],
            recv_sem=z_recv.at[k, d, h],
            device_id=((up, down)[d], tensor),
            device_id_type=MESH,
        )

    def home(k, values):
        if k in (0, count - 1):
            return conv_landed[k != 0].at[me]
        if k <= 2:
            at = lax.rem(me, 4)
            rows = pl.ds(pl.multiple_of(lax.rem(at, 2) * 16 + (k - 1) * 8, 8), 8)
            return (out_values if values else out_keys).at[:, rows, lanes(at // 2 * HEAD, HEAD)]
        return out_state.at[:, (k - 3) % 2 * 8 : (k - 3) % 2 * 8 + 8, lanes((k - 3) // 2 * RANKS * HEAD + me * HEAD, HEAD)]

    def gather_copy(k, o, values=False):
        return pltpu.make_async_remote_copy(
            src_ref=gathered[k].at[pl.ds(peers[o] * each, each)],
            dst_ref=home(k, values),
            send_sem=c_send.at[k, o],
            recv_sem=c_recv.at[k, o],
            device_id=partner[o],
            device_id_type=MESH,
        )

    def gather_self(k, values=False):
        return pltpu.make_async_copy(
            gathered[k].at[pl.ds(me * each, each)], home(k, values), c_self.at[k]
        )

    def begin(k):
        for o in range(1, RANKS):
            spread_copy(k, o).start()
        spread_self(k).start()

    def pack(k):
        for o in range(1, RANKS):
            spread_copy(k, o).wait_recv()
        spread_self(k).wait()

        @pl.loop(0, 2 * CAPS[0] // 8)
        def _(s):
            for u in range(8):
                at = s * 8 + u
                queue[k][at] = spread[k][tab[0, at]]

        for d in range(2):
            ring_copy(k, d, 0).start()

    def forward(k, h):
        for d in range(2):
            ring_copy(k, d, h - 1).wait_recv()
            ring_copy(k, d, h).start()

    def unpack(k):
        for d in range(2):
            ring_copy(k, d, 3).wait_recv()

        @pl.loop(0, width // 8)
        def _(s):
            for u in range(8):
                at = s * 8 + u
                gathered[k][at] = jnp.where(
                    tab[3, at] == 1, spread[k][tab[1, at]], ring[k][tab[2, at]]
                )

        def send(values):
            for o in range(1, RANKS):
                gather_copy(k, o, values).start()
            gather_self(k, values).start()

        if 1 <= k <= 2:
            pl.when(me < 4)(lambda: send(False))
            pl.when(me >= 4)(lambda: send(True))
        else:
            send(False)

    def wait_home(k):
        for o in range(1, RANKS):
            gather_copy(k, o).wait_recv()
        gather_self(k).wait()

    requests = each
    channels = conv_out.shape[1]
    steps = conv_out.shape[0] // requests

    def stage_conv():
        load("old").wait()
        load("fresh").wait()
        lines = [mem["old"].at[mem["old"].shape[0] - 1]] + [mem["fresh"].at[s] for s in range(steps)]
        for n, k in enumerate((0, count - 1)):
            for q in range(RANKS):
                at = (q * 2 + n) * HEAD
                for t, line in enumerate(lines):
                    loose[n, q, :, t, :] = line[:, at : at + HEAD].astype(jnp.float32)
                staged[k][q] = loose[n, q].astype(staged[k].dtype)

    def land_conv(n):
        for q in range(RANKS):
            at = (q * 2 + n) * HEAD
            loose[n, q] = conv_landed[n][q].astype(jnp.float32)
            for t in range(conv_final.shape[0]):
                conv_final[t, :, at : at + HEAD] = loose[n, q, :, t, :].astype(conv_final.dtype)

    def flatten():
        for name, row in zip(("conv_bias", "dt_gain", "dt_bias", "skip"), flat):
            load(name).wait()
            for n in range(mem[name].shape[0]):
                row[:, n * HEAD : (n + 1) * HEAD] = mem[name][n : n + 1, :]

    conv_bias, dt_gain, dt_bias, skip = flat

    def update_caches():
        load("key_new").wait()
        load("value_new").wait()
        key_fresh[...] = mem["key_new"][...].astype(jnp.float32)
        value_fresh[...] = mem["value_new"][...].astype(jnp.float32)
        load("key_cache").wait()
        load("value_cache").wait()

        @pl.loop(0, requests // 8)
        def _(block):
            ats = [pl.ds(pl.multiple_of(s * requests + block * 8, 8), 8) for s in range(steps)]
            for base, cache, fresh in ((0, mem["key_cache"], key_fresh), (4, mem["value_cache"], value_fresh)):
                for g in range(2):
                    cols = slice(g * HEAD, (g + 1) * HEAD)
                    new = [fresh[at, cols] for at in ats]
                    for u in range(8):
                        r = block * 8 + u
                        for p in range(2):
                            rows = lax.broadcasted_iota(jnp.int32, (16, HEAD), 0) + p * 16
                            tile = cache[r, p * 16 : p * 16 + 16, cols].astype(jnp.float32)
                            for s in range(steps):
                                tile = jnp.where(rows == kv_len[r] + s, new[s][u : u + 1], tile)
                            tile = tile.astype(caches.dtype)
                            caches[base + g * 2 + p, r] = tile
                            staged[1][base + g * 2 + p, r] = tile[:8]
                            staged[2][base + g * 2 + p, r] = tile[8:]

    def convolve():
        load("conv_weight").wait()
        taps = mem["conv_weight"].shape[0]
        window = [(mem["old"], n) for n in range(taps - 1)] + [(mem["fresh"], n) for n in range(steps)]

        @pl.loop(0, channels // 256)
        def _(b):
            cols = pl.ds(pl.multiple_of(b * 256, 256), 256)
            for s in range(steps):
                total_in = conv_bias[:, cols]
                for k in range(taps):
                    source, n = window[s + k]
                    line = source[n, :, cols].astype(jnp.float32)
                    total_in = total_in + mem["conv_weight"][k : k + 1, cols] * line
                conv_out[s * requests : (s + 1) * requests, cols] = silu(total_in).astype(conv_out.dtype)

    def share_copies(o):
        return [
            pltpu.make_async_remote_copy(
                src_ref=buf.at[tensor],
                dst_ref=buf.at[tensor],
                send_sem=p_send.at[n, o],
                recv_sem=p_recv.at[n, o],
                device_id=beside[o],
                device_id_type=MESH,
            )
            for n, buf in enumerate((low_parts, gain_parts))
        ]

    rank_width = low_parts.shape[2]
    state_width = gains.shape[1] // 2
    nt = (((1,), (1,)), ((), ()))

    def project():
        load("xproj").wait()
        low_parts[tensor] = lax.dot_general(
            conv_out[...], mem["xproj"][:rank_width], nt, preferred_element_type=jnp.float32
        )
        gain_parts[tensor, :, : steps * requests] = lax.dot_general(
            mem["xproj"][rank_width:], conv_out[...], nt, preferred_element_type=jnp.float32
        )
        for o in range(1, tensors):
            for copy in share_copies(o):
                copy.start()

    def rates():
        for o in range(1, tensors):
            for copy in share_copies(o):
                copy.wait_recv()
        low = low_parts[0]
        both = gain_parts[0]
        for t in range(1, tensors):
            low = low + low_parts[t]
            both = both + gain_parts[t]
        load("dtproj").wait()
        mean = jnp.mean(low * low, axis=-1, keepdims=True)
        scaled = (low * lax.rsqrt(mean + epsilon) * dt_gain[...]).astype(conv_out.dtype)
        for b in range(channels // 512):
            cols = slice(b * 512, (b + 1) * 512)
            rate = (
                jnp.dot(scaled, mem["dtproj"][:, cols], preferred_element_type=jnp.float32)
                + dt_bias[:, cols]
            )
            rate = jnp.maximum(rate, 0.0) + jnp.log1p(jnp.exp(-jnp.abs(rate)))
            delta[:, cols] = rate
            push[:, cols] = rate * conv_out[:, cols].astype(jnp.float32)
        for c in range(steps * requests):
            gains[c] = jnp.broadcast_to(both[:, c : c + 1], (2 * state_width, HEAD))

    def recur(half):
        @pl.loop(0, requests // 8 * 4)
        def _(turn):
            block, b = turn // 4, lax.rem(turn, 4)
            cols = pl.ds(pl.multiple_of(half * RANKS * HEAD + b * 256, 256), 256)
            ats = [pl.ds(pl.multiple_of(s * requests + block * 8, 8), 8) for s in range(steps)]
            decay = mem["decay"][:, cols]
            rates_now = [delta[at, cols] for at in ats]
            push_now = [push[at, cols] for at in ats]
            read = [[] for _ in ats]
            for u in range(8):
                r = block * 8 + u
                hidden = mem["state"][r, :, cols].astype(jnp.float32)
                for s in range(steps):
                    gain_in = gains[s * requests + r, :state_width]
                    gain_out = gains[s * requests + r, state_width:]
                    gain_in = jnp.concatenate([gain_in, gain_in], axis=1)
                    gain_out = jnp.concatenate([gain_out, gain_out], axis=1)
                    hidden = (
                        jnp.exp(-rates_now[s][u : u + 1] * decay) * hidden
                        + push_now[s][u : u + 1] * gain_in
                    )
                    read[s].append(jnp.sum(hidden * gain_out, axis=0, keepdims=True))
                final = hidden.astype(conv_out.dtype)
                for n in range(2):
                    for at in range(2):
                        staged[3 + 2 * half + at][2 * b + n, r] = final[
                            at * 8 : at * 8 + 8, n * HEAD : (n + 1) * HEAD
                        ]
            for s in range(steps):
                reading[ats[s], cols] = jnp.concatenate(read[s])

    def gate():
        load("gate").wait()

        @pl.loop(0, channels // 256)
        def _(b):
            cols = pl.ds(pl.multiple_of(b * 256, 256), 256)
            for s in range(steps):
                rows = slice(s * requests, (s + 1) * requests)
                read = reading[rows, cols] + skip[:, cols] * conv_out[rows, cols].astype(jnp.float32)
                mamba[s, :, cols] = (read * silu(mem["gate"][s, :, cols].astype(jnp.float32))).astype(mamba.dtype)

        pltpu.make_async_copy(mamba, out_mamba, o_sem.at[0]).start()

    group = mem["query"].shape[2] // HEAD // 2

    def attend(half, g):
        rows16 = slice(half * 16, half * 16 + 16)
        query = jnp.concatenate(
            [
                mem["query"][s, rows16, (g * group + h) * HEAD : (g * group + h + 1) * HEAD]
                for s in range(steps)
                for h in range(group)
            ]
        )
        size = query.shape[0]
        row = lax.broadcasted_iota(jnp.int32, (size, 256), 0)
        col = lax.broadcasted_iota(jnp.int32, (size, 256), 1)
        limit = lengths[half : half + 1, :] + row // (size // steps)
        scores = []
        for p in range(2):
            keys = caches[g * 2 + p, rows16].reshape(256, HEAD)
            score = lax.dot_general(query, keys, nt, preferred_element_type=jnp.float32) / math.sqrt(HEAD)
            allowed = (row % 16 == col // 16) & (col % 16 + p * 16 <= limit)
            scores.append(jnp.where(allowed, score, -1e30))
        highest = jnp.maximum(
            jnp.max(scores[0], axis=-1, keepdims=True), jnp.max(scores[1], axis=-1, keepdims=True)
        )
        weights = [jnp.exp(score - highest) for score in scores]
        whole = jnp.sum(weights[0], axis=-1, keepdims=True) + jnp.sum(weights[1], axis=-1, keepdims=True)
        inverse = 1.0 / whole
        mixed = jnp.zeros((size, HEAD), jnp.float32)
        for p in range(2):
            values = caches[4 + g * 2 + p, rows16].reshape(256, HEAD)
            mixed = mixed + jnp.dot(
                (weights[p] * inverse).astype(values.dtype), values, preferred_element_type=jnp.float32
            )
        mixed = mixed.astype(attn.dtype)
        for s in range(steps):
            for h in range(group):
                at = (s * group + h) * 16
                attn[s, rows16, (g * group + h) * HEAD : (g * group + h + 1) * HEAD] = mixed[at : at + 16]

    def attention(half, g):
        if half == 0 and g == 0:
            load("query").wait()
            lane_request = lax.broadcasted_iota(jnp.int32, lengths.shape, 1) // 16
            lane_request = lane_request + 16 * lax.broadcasted_iota(jnp.int32, lengths.shape, 0)
            found = jnp.zeros(lengths.shape, jnp.int32)
            for r in range(requests):
                found = jnp.where(lane_request == r, kv_len[r], found)
            lengths[...] = found
        attend(half, g)

    def recurrence(half):
        if half == 0:
            load("decay").wait()
            load("state").wait()
        recur(half)
        begin(3 + 2 * half)
        begin(4 + 2 * half)
        if half == 1:
            begin(count - 1)

    stage_conv()
    pl.semaphore_wait(barrier, len(friends))
    begin(0)
    update_caches()
    begin(1)
    begin(2)
    flatten()
    convolve()
    project()
    pack(0)
    attention(0, 0)
    pack(1)
    attention(1, 0)
    rates()
    pack(2)
    recurrence(0)
    forward(0, 1)
    recurrence(1)
    forward(1, 1)
    forward(0, 2)
    attention(0, 1)
    pack(3)
    forward(2, 1)
    attention(1, 1)
    pltpu.make_async_copy(attn, out_attn, o_sem.at[1]).start()
    forward(1, 2)
    forward(0, 3)
    gate()
    for step in range(4, count + 4):
        for stage in (4, 3, 2, 1, 0):
            k = step - stage
            if 0 <= k < count:
                if stage == 0:
                    pack(k)
                elif stage == 4:
                    unpack(k)
                else:
                    forward(k, stage)
        if step == 6:
            wait_home(0)
            land_conv(0)

    wait_home(count - 1)
    land_conv(1)
    pltpu.make_async_copy(conv_final, out_conv, o_sem.at[2]).start()
    for k in range(1, count - 1):
        wait_home(k)
    pltpu.make_async_copy(conv_final, out_conv, o_sem.at[2]).wait()
    pltpu.make_async_copy(mamba, out_mamba, o_sem.at[0]).wait()
    pltpu.make_async_copy(attn, out_attn, o_sem.at[1]).wait()
    for k in range(count):
        for o in range(1, RANKS):
            spread_copy(k, o).wait_send()
            gather_copy(k, o).wait_send()
        for d in range(2):
            for h in range(4):
                ring_copy(k, d, h).wait_send()
    for o in range(1, tensors):
        for copy in share_copies(o):
            copy.wait_send()


def deliver_kernel(*refs):
    count = (len(refs) - 2) // 3
    in_sem, out_sem = refs[-2:]
    first, second = [], []
    for n in range(count):
        source, target, middle = refs[n], refs[count + n], refs[2 * count + n]
        lead = source.shape[0]
        cuts = 4 if lead % 4 == 0 else lead
        for cut in range(cuts):
            rows = pl.ds(cut * (lead // cuts), lead // cuts)
            first.append(pltpu.make_async_copy(source.at[rows], middle.at[rows], in_sem.at[n, cut]))
            second.append(pltpu.make_async_copy(middle.at[rows], target.at[rows], out_sem.at[n, cut]))
    for copy in first:
        copy.start()
    for before, after in zip(first, second):
        before.wait()
        after.start()
    for copy in second:
        copy.wait()


def deliver(arrays):
    anywhere = pl.BlockSpec(memory_space=pl.ANY)
    return pl.pallas_call(
        deliver_kernel,
        out_shape=[jax.ShapeDtypeStruct(a.shape, a.dtype) for a in arrays],
        in_specs=[anywhere] * len(arrays),
        out_specs=[anywhere] * len(arrays),
        scratch_shapes=[pltpu.VMEM(a.shape, a.dtype) for a in arrays]
        + [pltpu.SemaphoreType.DMA((len(arrays), 4))] * 2,
        compiler_params=pltpu.CompilerParams(vmem_limit_bytes=56 * 2**20),
    )(*arrays)


def fast_steps(number, caps, tables, kv_length, loads, outs):
    taps, requests, channels = outs[2]
    steps = loads["query"].shape[0]
    width = RANKS * requests
    kind = loads["query"].dtype
    slices = [(4, HEAD)] + [(8, HEAD)] * 6 + [(4, HEAD)]
    count = len(slices)
    rank_width = loads["dtproj"].shape[0]
    gains = loads["xproj"].shape[0] - rank_width
    rows = steps * requests
    tensors = lax.axis_size("tensor")
    smem = pl.BlockSpec(memory_space=pltpu.SMEM)
    anywhere = pl.BlockSpec(memory_space=pl.ANY)
    f32 = jnp.float32
    scratch = [pltpu.VMEM(loads[name].shape, loads[name].dtype) for name in LOADS]
    for slots in (width, 2 * CAPS[0], 2 * sum(CAPS), width):
        scratch += [pltpu.VMEM((slots,) + each, kind) for each in slices]
    scratch += [pltpu.VMEM((RANKS, requests) + each, kind) for each in slices]
    scratch += [
        pltpu.VMEM((RANKS, requests, 16, HEAD), kind),
        pltpu.VMEM((2, RANKS, requests) + slices[0], f32),
        pltpu.VMEM((RANKS, requests) + slices[0], kind),
        pltpu.VMEM((RANKS, requests) + slices[-1], kind),
        pltpu.VMEM((taps, requests, channels), kind),
        pltpu.VMEM((2, 16 * requests // 2), jnp.int32),
        pltpu.VMEM(loads["key_new"].shape, f32),
        pltpu.VMEM(loads["value_new"].shape, f32),
        pltpu.VMEM((rows, channels), kind),
        pltpu.VMEM((tensors, rows, rank_width), f32),
        pltpu.VMEM((tensors, gains, HEAD), f32),
        pltpu.VMEM((rows, channels), f32),
        pltpu.VMEM((rows, channels), f32),
        pltpu.VMEM((rows, channels), f32),
        pltpu.VMEM((rows, gains, HEAD), f32),
        pltpu.VMEM((steps, requests, channels), kind),
        pltpu.VMEM((steps, requests, channels), kind),
    ]
    scratch += [
        pltpu.VMEM((1, loads[name].size), f32) for name in ("conv_bias", "dt_gain", "dt_bias", "skip")
    ]
    dma = pltpu.SemaphoreType.DMA
    scratch += [
        dma((len(LOADS),)),
        dma((count, RANKS)),
        dma((count, RANKS)),
        dma((count,)),
        dma((count, 2, 4)),
        dma((count, 2, 4)),
        dma((count, RANKS)),
        dma((count, RANKS)),
        dma((count,)),
        dma((2, tensors)),
        dma((2, tensors)),
        dma((3,)),
    ]
    return pl.pallas_call(
        functools.partial(step_kernel, count, caps),
        out_shape=[jax.ShapeDtypeStruct(shape, kind) for shape in outs],
        in_specs=[smem, smem] + [anywhere] * len(LOADS),
        out_specs=[anywhere] * 6,
        scratch_shapes=scratch,
        compiler_params=pltpu.CompilerParams(
            collective_id=number, has_side_effects=True, vmem_limit_bytes=56 * 2**20
        ),
    )(tables, kv_length, *[loads[name] for name in LOADS])


def project_rows(conv_rows, xproj_weight):
    return lax.dot_general(
        conv_rows, xproj_weight, (((1,), (1,)), ((), ())), preferred_element_type=jnp.float32
    )


def slot_ranks(owners):
    slot_count = owners.shape[-1]
    slot_order = jnp.arange(slot_count, dtype=jnp.int32)
    earlier = slot_order[None, :] < slot_order[:, None]
    matching = owners[..., :, None] == owners[..., None, :]
    return jnp.sum(jnp.where(matching & earlier, 1, 0), axis=-1).astype(jnp.int32)


def pack_slots(values_in, send_slots, total_slots):
    return (
        jnp.zeros((total_slots,) + values_in.shape[1:], values_in.dtype)
        .at[send_slots]
        .set(values_in)
    )


def exchange(new_owner, arrays):
    requests_here = arrays[0].shape[0]
    sections = lax.axis_size("section")
    section_index = lax.axis_index("section")
    capacity = max(1, requests_here // sections)
    total_slots = sections * capacity
    owners = new_owner.reshape(sections, requests_here)
    my_owners = lax.dynamic_slice_in_dim(owners, section_index, 1, 0)[0]
    send_slots = my_owners * capacity + slot_ranks(my_owners)
    ranks_all = slot_ranks(owners)
    arriving = owners == section_index
    sources = jnp.arange(sections, dtype=jnp.int32)[:, None]
    recv_slots = jnp.sum(jnp.where(arriving, sources * capacity + ranks_all, 0), axis=0)
    def select(places, options, rows):
        chosen = (places[:, None] == jnp.arange(options)[None, :]).astype(rows.dtype)
        flat = rows.reshape(rows.shape[0], -1)
        picked = jnp.dot(chosen, flat, preferred_element_type=jnp.float32)
        return picked.astype(rows.dtype).reshape((places.shape[0],) + rows.shape[1:])

    return tuple(
        select(
            recv_slots,
            total_slots,
            lax.all_to_all(
                pack_slots(array, send_slots, total_slots),
                "section",
                split_axis=0,
                concat_axis=0,
                tiled=True,
            ),
        )
        for array in arrays
    )


def plain_steps(
    inner_input,
    gate_input,
    conv_state,
    mamba_state,
    conv_weight,
    conv_bias,
    xproj_weight,
    dt_gain,
    dtproj_weight,
    dt_bias,
    decay_rate,
    skip_gain,
    query,
    key_cache,
    value_cache,
    key_new,
    value_new,
    kv_length,
    new_owner,
):
    steps_count = inner_input.shape[0]
    requests_here = inner_input.shape[1]
    channels = inner_input.shape[2]
    tap_count = conv_weight.shape[0]
    rank_width = dt_gain.shape[0]
    state_width = mamba_state.shape[1]
    tensors = lax.axis_size("tensor")
    window = jnp.concatenate([conv_state, jnp.swapaxes(inner_input, 0, 1)], axis=1)
    conv_list = []
    for step_index in range(steps_count):
        summed = jnp.zeros((requests_here, channels), jnp.float32) + conv_bias
        for tap_index in range(tap_count):
            summed = summed + conv_weight[tap_index] * window[:, step_index + tap_index].astype(
                jnp.float32
            )
        conv_list.append(jax.nn.silu(summed).astype(jnp.bfloat16))
    conv_out = jnp.stack(conv_list)
    hidden = mamba_state.astype(jnp.float32)
    mamba_list = []
    for step_index in range(steps_count):
        partial = project_rows(conv_out[step_index], xproj_weight)
        projected = partial
        for shift in range(1, tensors):
            pairs = [(source, (source + shift) % tensors) for source in range(tensors)]
            projected = projected + lax.ppermute(partial, "tensor", pairs)
        low_rank = projected[:, :rank_width]
        scaled = (
            low_rank
            * lax.rsqrt(jnp.mean(low_rank * low_rank, axis=-1, keepdims=True) + epsilon)
            * dt_gain
        ).astype(jnp.bfloat16)
        delta_rate = jax.nn.softplus(
            jnp.dot(scaled, dtproj_weight, preferred_element_type=jnp.float32) + dt_bias
        )
        input_gain = projected[:, rank_width : rank_width + state_width]
        output_gain = projected[:, rank_width + state_width :]
        inputs_now = conv_out[step_index].astype(jnp.float32)
        hidden = (
            jnp.exp(-delta_rate[:, None, :] * decay_rate[None]) * hidden
            + (delta_rate * inputs_now)[:, None, :] * input_gain[:, :, None]
        )
        reading = jnp.sum(hidden * output_gain[:, :, None], axis=1) + skip_gain * inputs_now
        mamba_list.append(
            (reading * jax.nn.silu(gate_input[step_index].astype(jnp.float32))).astype(jnp.bfloat16)
        )
    final_state = hidden.astype(jnp.bfloat16)
    final_conv = window[:, steps_count:]
    cache_slots = key_cache.shape[1]
    cache_heads = key_cache.shape[2] // HEAD
    query_heads = query.shape[2] // HEAD
    group_size = query_heads // cache_heads
    positions = jnp.arange(cache_slots, dtype=jnp.int32)
    key_rows = key_cache
    value_rows = value_cache
    attended = []
    for step_index in range(steps_count):
        target = kv_length + step_index
        written = (positions[None, :] == target[:, None])[:, :, None]
        key_rows = jnp.where(written, key_new[step_index][:, None, :], key_rows)
        value_rows = jnp.where(written, value_new[step_index][:, None, :], value_rows)
        queries = query[step_index].reshape(requests_here, cache_heads, group_size, HEAD)
        key_heads = key_rows.reshape(requests_here, cache_slots, cache_heads, HEAD)
        scores = jnp.einsum(
            "rgqd,rcgd->rgqc", queries, key_heads, preferred_element_type=jnp.float32
        ) / math.sqrt(HEAD)
        allowed = (positions[None, :] <= target[:, None])[:, None, None, :]
        scores = jnp.where(allowed, scores, -1e30)
        highest = jnp.max(scores, axis=-1, keepdims=True)
        weights = jnp.exp(scores - highest)
        weights = (weights / jnp.sum(weights, axis=-1, keepdims=True)).astype(jnp.bfloat16)
        value_heads = value_rows.reshape(requests_here, cache_slots, cache_heads, HEAD)
        mixed_out = jnp.einsum(
            "rgqc,rcgd->rgqd", weights, value_heads, preferred_element_type=jnp.float32
        )
        attended.append(mixed_out.reshape(requests_here, query_heads * HEAD).astype(jnp.bfloat16))
    arrays = (final_conv, final_state, key_rows, value_rows)
    moved = exchange(new_owner, arrays)
    return (jnp.stack(mamba_list), jnp.stack(attended), *moved)


def local(
    inner_input,
    gate_input,
    conv_state,
    mamba_state,
    conv_weight,
    conv_bias,
    xproj_weight,
    dt_gain,
    dtproj_weight,
    dt_bias,
    decay_rate,
    skip_gain,
    query,
    key_cache,
    value_cache,
    key_new,
    value_new,
    kv_length,
    new_owner,
):
    steps, requests, channels = inner_input.shape
    positions, width = key_cache.shape[1:]
    tables = route_tables(new_owner)
    loads = {
        "key_cache": key_cache,
        "value_cache": value_cache,
        "key_new": key_new.reshape(steps * requests, width),
        "value_new": value_new.reshape(steps * requests, width),
        "old": jnp.swapaxes(conv_state, 0, 1),
        "fresh": inner_input,
        "conv_weight": conv_weight,
        "conv_bias": conv_bias.reshape(-1, HEAD),
        "xproj": xproj_weight,
        "query": query,
        "dt_gain": dt_gain.reshape(-1, HEAD),
        "dtproj": dtproj_weight,
        "dt_bias": dt_bias.reshape(-1, HEAD),
        "decay": decay_rate,
        "state": mamba_state,
        "gate": gate_input,
        "skip": skip_gain.reshape(-1, HEAD),
    }
    outs = [
        inner_input.shape,
        query.shape,
        loads["old"].shape,
        mamba_state.shape,
        key_cache.shape,
        value_cache.shape,
    ]

    def fast(number, caps):
        moved = fast_steps(number, caps, tables, kv_length, loads, outs)
        mamba, attn, conv, *moved = deliver(moved)
        return (mamba, attn, jnp.swapaxes(conv, 0, 1), *moved)

    return lax.switch(
        tables[4, 0],
        [
            lambda: fast(0, TIGHT),
            lambda: fast(1, CAPS),
            lambda: plain_steps(
                inner_input,
                gate_input,
                conv_state,
                mamba_state,
                conv_weight,
                conv_bias,
                xproj_weight,
                dt_gain,
                dtproj_weight,
                dt_bias,
                decay_rate,
                skip_gain,
                query,
                key_cache,
                value_cache,
                key_new,
                value_new,
                kv_length,
                new_owner,
            ),
        ],
    )


def solution(mesh):
    in_specs = (
        P(None, "section", "tensor"),
        P(None, "section", "tensor"),
        P("section", None, "tensor"),
        P("section", None, "tensor"),
        P(None, "tensor"),
        P("tensor"),
        P(None, "tensor"),
        P(),
        P(None, "tensor"),
        P("tensor"),
        P(None, "tensor"),
        P("tensor"),
        P(None, "section", "tensor"),
        P("section", None, "tensor"),
        P("section", None, "tensor"),
        P(None, "section", "tensor"),
        P(None, "section", "tensor"),
        P("section"),
        P(),
    )
    out_specs = (
        P(None, "section", "tensor"),
        P(None, "section", "tensor"),
        P("section", None, "tensor"),
        P("section", None, "tensor"),
        P("section", None, "tensor"),
        P("section", None, "tensor"),
    )
    return jax.shard_map(local, mesh=mesh, in_specs=in_specs, out_specs=out_specs, check_vma=False)
```
